256 devices in a mesh: batch: 8 (over y, x_lo), train: 32 (over z, x_hi, core).
Axes of the slice: x: 4 (x_hi: 2, x_lo: 2; x = x_hi * 2 + x_lo), y: 4, z: 8, core: 2. Of those that a mesh axis runs over, the one named last changes fastest.
Arguments:
- batch_rows: int32 [2, 8192], replicated, may hold values from 0 to 131071, as said below
- train_embed: bfloat16 [131072, 256], P('train'), may hold values from -6 to 6
- lib_embed: bfloat16 [8192, 256], P('batch'), may hold values from -6 to 6
- labels: float32 [131072], P('train'), may hold values from -6 to 6
- prior_draws: float32 [32, 131072], P(None, 'train'), may hold values from -6 to 6
- noise_draws: float32 [32, 131072], P(None, 'train'), may hold values from -6 to 6
- coefficients: float32 [33, 131072], P(None, 'train'), may hold values from -4 to 4
- velocity: float32 [33, 131072], P(None, 'train'), may hold values from -1.6 to 1.6
- library_prior: float32 [32, 8192], P(None, ('batch', 'train')), may hold values from -6 to 6
Outputs:
- new_coefficients: float32 [33, 131072], P(None, 'train')
- new_velocity: float32 [33, 131072], P(None, 'train')
- predictions: float32 [33, 8192], P(None, ('batch', 'train'))
The draws below stay inside these ranges and needn't reach their ends.
Inputs may be any that keep to these rules, and one draw needn't show every extreme that they name: `batch_rows`: each step's 8192 rows are distinct. A step's positions fall into runs of 32; run number q holds rows of the range starting at (q % 32) * 4096 of length 4096.
All inputs are finite; a program needn't handle non-finite values.
Results may differ from the reference program's by a relative error of at most 0.009.
Values may be sent and summed in bfloat16 or wider, within the bound.
No kernel may reach another device: no remote copies, remote signals or barrier semaphores. Data moves between devices by JAX's collectives and lax.ppermute only.
A program may use at most 64 MiB of HBM per device.

```python
import jax
import jax.numpy as jnp
from jax import lax

D = 256
SAMPLES = 32
STEPS = 2
TRAIN_DEV = 4096
BATCH_DEV = 1024
N = 131072
BATCH = 8192
LIBRARY = 8192
OWN = 32
COLS = 33
CLUSTERS = 2048
N_TRAIN = 32


def family_centers(key):
    return jax.random.normal(jax.random.fold_in(key, 7), (CLUSTERS, D), jnp.float32)


def clustered(key, salt, count):
    centers = family_centers(key)
    member = jax.random.randint(jax.random.fold_in(key, salt), (count,), 0, CLUSTERS)
    spread = 0.315 * jax.random.normal(jax.random.fold_in(key, salt + 1), (count, D), jnp.float32)
    rows = jnp.take(centers, member, axis=0) + spread
    return jnp.clip(rows, -6.0, 6.0).astype(jnp.bfloat16)


def draw_train_embed(key, part):
    return clustered(key, 21, N)


def draw_lib_embed(key, part):
    return clustered(key, 31, LIBRARY)


def draw_batch_rows(key, part):
    shards = N // TRAIN_DEV
    groups = BATCH // BATCH_DEV
    picked_count = groups * OWN

    def one_step(step_index):
        step_key = jax.random.fold_in(key, 100 + step_index)

        def one_shard(shard):
            order = jax.random.permutation(jax.random.fold_in(step_key, shard), TRAIN_DEV)
            return order[:picked_count].reshape(groups, OWN) + shard * TRAIN_DEV
        table = jax.vmap(one_shard)(jnp.arange(shards, dtype=jnp.int32))
        return jnp.transpose(table, (1, 0, 2)).reshape(BATCH)
    return jnp.stack([one_step(step_index) for step_index in range(STEPS)]).astype(jnp.int32)


def shard_levels(own_key, extent, cuts, smallest, top_value):
    def one(axis_at, shards_of):
        steps = jax.random.uniform(jax.random.fold_in(jax.random.fold_in(own_key, 6), axis_at), (shards_of,), jnp.float32, smallest / len(cuts), top_value / len(cuts))
        return jnp.repeat(jnp.exp(steps), extent[axis_at] // shards_of).reshape((-1,) + (1,) * (len(extent) - axis_at - 1))

    loudness = one(*cuts[0])
    for cut in cuts[1:]:
        loudness = loudness * one(*cut)
    return loudness


def gaussian(rng, shape, scale, limit, cuts=(), kind=jnp.bfloat16):
    gain = shard_levels(rng, shape, cuts, -0.22, 0.18) if cuts else 1.0
    values = jax.random.normal(rng, shape, jnp.float32) * scale * gain
    return jnp.minimum(jnp.maximum(values, -limit), limit).astype(kind)


def setup_inputs(seed: int = 0) -> dict:
    splits = jax.random.split(jax.random.key(seed), 10)
    return {
        "batch_rows": draw_batch_rows(jax.random.fold_in(splits[9], 71), 0),
        "train_embed": draw_train_embed(jax.random.fold_in(splits[9], 71), 0),
        "lib_embed": draw_lib_embed(jax.random.fold_in(splits[9], 71), 0),
        "labels": gaussian(splits[3], (N,), 1.0, 6.0, ((0, 32),), jnp.float32),
        "prior_draws": gaussian(splits[4], (SAMPLES, N), 1.0, 6.0, ((1, 32),), jnp.float32),
        "noise_draws": gaussian(splits[5], (SAMPLES, N), 1.0, 6.0, ((1, 32),), jnp.float32),
        "coefficients": gaussian(splits[6], (COLS, N), 0.5, 4.0, ((1, 32),), jnp.float32),
        "velocity": gaussian(splits[7], (COLS, N), 0.2, 1.6, ((1, 32),), jnp.float32),
        "library_prior": gaussian(splits[8], (SAMPLES, LIBRARY), 1.0, 6.0, ((1, 256),), jnp.float32),
    }


momentum = 0.9
step_rate = 0.1
noise_var = 0.5
noise_scale = 0.7071067811865476
length_sq = 0.088

def contract_rows(left, right):
    return lax.dot_general(left, right, (((1,), (1,)), ((), ())), preferred_element_type=jnp.float32)

def kernel_tile(query, keys, key_norms, width):
    query_norms = lax.optimization_barrier(jnp.sum(jnp.square(query.astype(jnp.float32)), axis=1))
    cross = contract_rows(query, keys)
    dist = query_norms[:, None] + key_norms[None, :] - 2.0 * cross
    scaled = jnp.sqrt(5.0 * jnp.maximum(dist, 0.0) / (length_sq * width))
    return ((1.0 + scaled + scaled * scaled / 3.0) * jnp.exp(-scaled)).astype(jnp.bfloat16)

def apply_kernel(query, train_embed, weights):
    width = train_embed.shape[1]
    key_norms = lax.optimization_barrier(jnp.sum(jnp.square(train_embed.astype(jnp.float32)), axis=1))
    systems = weights.shape[0]

    def one_block(carry, parts):
        keys, norms, block_weights = parts
        tile = kernel_tile(query, keys, norms, width)
        return (carry + contract_rows(block_weights, tile), None)
    start = jnp.zeros((systems, query.shape[0]), jnp.float32)
    total, _ = lax.scan(one_block, start, (train_embed.reshape(N_TRAIN, TRAIN_DEV, width), key_norms.reshape(N_TRAIN, TRAIN_DEV), jnp.transpose(weights.reshape(systems, N_TRAIN, TRAIN_DEV), (1, 0, 2))))
    return total

def reference(batch_rows, train_embed, lib_embed, labels, prior_draws, noise_draws, coefficients, velocity, library_prior):
    targets = jnp.concatenate([labels[None, :], labels[None, :] - prior_draws - noise_scale * noise_draws], axis=0)
    for step_index in range(STEPS):
        chosen = batch_rows[step_index]
        ahead = coefficients + momentum * velocity
        query = jnp.take(train_embed, chosen, axis=0)
        resid = apply_kernel(query, train_embed, ahead.astype(jnp.bfloat16))
        resid = resid + noise_var * jnp.take(ahead, chosen, axis=1) - jnp.take(targets, chosen, axis=1)
        grad = jnp.zeros_like(coefficients).at[:, chosen].add(resid)
        velocity = momentum * velocity - step_rate * grad
        coefficients = coefficients + velocity
    predicted = apply_kernel(lib_embed, train_embed, coefficients.astype(jnp.bfloat16))
    shifts = jnp.concatenate([jnp.zeros((1, predicted.shape[1]), jnp.float32), library_prior], axis=0)
    return (coefficients, velocity, predicted + shifts)
```

```python
import functools

import jax
import jax.numpy as jnp
from jax import lax
from jax.experimental import pallas as pl
from jax.experimental.pallas import tpu as pltpu
from jax.sharding import PartitionSpec as P

momentum = 0.9
step_rate = 0.1
noise_var = 0.5
noise_scale = 0.7071067811865476
length_sq = 0.088

BETA = (5.0 / (length_sq * 256)) ** 0.5
SCALE = BETA * BETA / 3.0
C1 = 3.0 / BETA
C0 = 3.0 / (BETA * BETA)
RATE = BETA * 1.4426950408889634

CARRY = momentum + momentum * momentum
CUT = step_rate * (1.0 + momentum)

ROWS = 48
f32 = jnp.float32
bf16 = jnp.bfloat16

VMEM = pl.BlockSpec(memory_space=pltpu.VMEM)
SMEM = pl.BlockSpec(memory_space=pltpu.SMEM)


def call(body, outs, *args, name, flops=0, scratch=(), smem=0):
    return pl.pallas_call(
        body,
        out_shape=outs,
        in_specs=[SMEM] * smem + [VMEM] * (len(args) - smem),
        out_specs=jax.tree.map(lambda _: VMEM, outs),
        scratch_shapes=list(scratch),
        compiler_params=pltpu.CompilerParams(vmem_limit_bytes=40 << 20),
        cost_estimate=pl.CostEstimate(
            flops=flops, transcendentals=0, bytes_accessed=sum(a.size * a.dtype.itemsize for a in args)
        ),
        name=name,
    )(*args)


def shaped(shape, dtype):
    return jax.ShapeDtypeStruct(shape, dtype)


def dot_nt(left, right):
    return lax.dot_general(left, right, (((1,), (1,)), ((), ())), preferred_element_type=f32)


def dot_nn(left, right):
    return jnp.dot(left, right, preferred_element_type=f32)


def two_terms(x):
    high = x.astype(bf16)
    return high, (x - high.astype(f32)).astype(bf16)


def row_norms(x):
    return jnp.sum(jnp.square(x.astype(f32)), axis=1, keepdims=True)


def norms_on_lanes(x):
    wide = jnp.broadcast_to(row_norms(x), (x.shape[0], 128))
    return jnp.transpose(wide)[0:1, :]


def matern(cross, key_norms, query_norms):
    dist = jnp.maximum((key_norms + query_norms) + cross, 1e-12)
    root = dist * lax.rsqrt(dist)
    return ((root * (root + C1) + C0) * jnp.exp2(root * -RATE)).astype(bf16)


def own_columns(rows_ref, batch, train, spread):
    per_batch = 1024
    chunks = []
    for step in range(2):
        for group in range(8) if spread else (batch,):
            start = group * per_batch + (train // 4) * 128
            chunks.append(rows_ref[pl.ds(step, 1), pl.ds(pl.multiple_of(start, 128), 128)])
    while len(chunks) % 8:
        chunks.append(chunks[0])
    stack = jnp.concatenate(chunks, axis=0)
    stack = pltpu.roll(stack, lax.rem(128 - (train % 4) * 32, 128), axis=1)
    return stack - train * 4096


def pick_body(place_ref, rows_ref, embed_ref, out_ref):
    batch, train = place_ref[0], place_ref[1]
    local = jnp.transpose(own_columns(rows_ref, batch, train, False))
    lanes = lax.broadcasted_iota(jnp.int32, (32, 4096), 1)
    for step in range(2):
        chosen = (lanes == local[0:32, step : step + 1]).astype(bf16)
        out_ref[step] = dot_nn(chosen, embed_ref[...]).astype(bf16)


def packed(x):
    return jnp.concatenate([x[0:16], x[16:32], x[32:48], jnp.zeros((16, 32), x.dtype)], axis=1)


def unpacked(x):
    return jnp.concatenate([x[:, 0:32], x[:, 32:64], x[:, 64:96]], axis=0)


def prep_body(
    place_ref, rows_ref, embed_ref, labels_ref, prior_ref, noise_ref, coef_ref, vel_ref,
    ahead_ref, base_ref, own_ref, picks_ref, norms_ref, same_ref, local_ref,
):
    batch, train = place_ref[0], place_ref[1]
    coef = coef_ref[...]
    vel = vel_ref[...]
    ahead = coef + momentum * vel
    base = coef + CARRY * vel
    shift = jnp.concatenate(
        [jnp.zeros((1, 4096), f32), prior_ref[...] + noise_scale * noise_ref[...]], axis=0
    )
    targets = labels_ref[...] - shift
    pad = jnp.zeros((ROWS - 33, 4096), f32)
    ahead_ref[...] = jnp.concatenate([ahead, pad], axis=0).astype(bf16)
    base_ref[...] = jnp.concatenate([base, pad], axis=0).astype(bf16)
    mine = jnp.transpose(own_columns(rows_ref, batch, train, False))
    lanes = lax.broadcasted_iota(jnp.int32, (32, 4096), 1)
    for step, state in enumerate((ahead, base)):
        chosen = (lanes == mine[0:32, step : step + 1]).astype(bf16)
        high, low = two_terms(jnp.concatenate([noise_var * state - targets, pad], axis=0))
        own_ref[step] = packed(dot_nt(high, chosen) + dot_nt(low, chosen))
    spread = own_columns(rows_ref, batch, train, True)
    every = jnp.transpose(spread)
    local_ref[...] = every
    for index in range(16):
        chosen = (lanes == every[0:32, index : index + 1]).astype(bf16)
        picks_ref[32 * index : 32 * index + 32, :] = dot_nn(chosen, embed_ref[...]).astype(bf16)
    norms_ref[...] = row_norms(embed_ref[...])
    first = mine[0:32, 0:1]
    for group in range(8):
        same_ref[:, 32 * group : 32 * group + 32] = (
            first == spread[8 + group : 9 + group, 0:32]
        ).astype(f32) * (noise_var / SCALE)


KEY_TILE = 1024
QUERY_TILE = 256


def dense(embed_ref, query_ref, norms_ref, weight_ref, out_ref, cross_ref):
    key_count, query_count = embed_ref.shape[0], query_ref.shape[0]
    query_tiles = query_count // QUERY_TILE
    tiles = (key_count // KEY_TILE) * query_tiles

    def window(tile):
        key_at = pl.multiple_of((tile // query_tiles) * KEY_TILE, KEY_TILE)
        query_at = pl.multiple_of((tile % query_tiles) * QUERY_TILE, QUERY_TILE)
        return pl.ds(key_at, KEY_TILE), pl.ds(query_at, QUERY_TILE)

    def cross(tile):
        keys, queries = window(tile)
        return dot_nt(embed_ref[keys, :], query_ref[queries, :] * bf16(-2))

    out_ref[...] = jnp.zeros_like(out_ref)
    query_norms = norms_on_lanes(query_ref[...])
    cross_ref[2, 0:8, 0:256] = jnp.broadcast_to(query_norms[:, 0:256], (8, 256))
    cross_ref[2, 8:16, 0:256] = jnp.broadcast_to(query_norms[:, 256:512], (8, 256))
    cross_ref[2, 16:24, 0:256] = jnp.broadcast_to(query_norms[:, 512:768], (8, 256))
    cross_ref[2, 24:32, 0:256] = jnp.broadcast_to(query_norms[:, 768:1024], (8, 256))
    cross_ref[0] = cross(0)

    def one(tile, slot):
        cross_ref[1 - slot] = cross(jnp.minimum(tile + 1, tiles - 1))
        keys, queries = window(tile)
        at = pl.multiple_of((tile % query_tiles) * 8, 8)
        value = matern(cross_ref[slot], norms_ref[keys, :], cross_ref[2, pl.ds(at, 8), :][0:1, :])
        out_ref[:, queries] += dot_nn(weight_ref[:, keys], value)

    def pair(index, carry):
        one(2 * index, 0)
        one(2 * index + 1, 1)
        return carry

    lax.fori_loop(0, tiles // 2, pair, 0)
    out_ref[...] *= SCALE


def pack_for_train(total, out_ref):
    lane = lax.broadcasted_iota(jnp.int32, (16, 128), 1) // 32
    for group in range(8):
        for place in range(4):
            block = jnp.zeros((16, 128), f32)
            for band in range(3):
                part = total[16 * band : 16 * band + 16, 128 * group : 128 * group + 128]
                moved = (32 * (band - place)) % 128
                if moved:
                    part = pltpu.roll(part, moved, axis=1)
                block = jnp.where(lane == band, part, block)
            out_ref[4 * group + place] = block.astype(bf16)


def unpack_from_train(blocks):
    lane = lax.broadcasted_iota(jnp.int32, (16, 128), 1) // 32
    bands = []
    for band in range(3):
        groups = []
        for group in range(8):
            wide = jnp.zeros((16, 128), f32)
            for place in range(4):
                part = blocks[4 * group + place]
                moved = (32 * (place - band)) % 128
                if moved:
                    part = pltpu.roll(part, moved, axis=1)
                wide = jnp.where(lane == place, part, wide)
            groups.append(wide)
        bands.append(jnp.concatenate(groups, axis=1))
    return jnp.concatenate(bands, axis=0)


def dense_batch_body(embed_ref, query_ref, norms_ref, weight_ref, out_ref, cross_ref, total_ref):
    dense(embed_ref, query_ref, norms_ref, weight_ref, total_ref, cross_ref)
    pack_for_train(total_ref[...], out_ref)


def dense_library_body(
    embed_ref, query_ref, norms_ref, weight_ref, picks_ref, out_ref, near_ref, cross_ref
):
    query_norms = norms_on_lanes(query_ref[...])
    for index in range(2):
        picks = picks_ref[256 * index : 256 * index + 256, :]
        near_ref[256 * index : 256 * index + 256, :] = matern(
            dot_nt(picks, query_ref[...] * bf16(-2)), row_norms(picks), query_norms
        )
    dense(embed_ref, query_ref, norms_ref, weight_ref, out_ref, cross_ref)


def between_body(place_ref, first_ref, picks_ref, same_ref, out_ref):
    train = place_ref[1]
    picks = picks_ref[256:512, :]
    pick_norms = norms_on_lanes(picks)
    for index in range(4):
        queries = first_ref[256 * index : 256 * index + 256, :]
        out_ref[256 * index : 256 * index + 256, :] = matern(
            dot_nt(queries * bf16(-2), picks), row_norms(queries), pick_norms
        )
    mine = pl.ds(pl.multiple_of(train * 32, 32), 32)
    out_ref[mine, :] = (out_ref[mine, :].astype(f32) + same_ref[...]).astype(bf16)


def first_body(arrived_ref, own_ref, second_ref, out_ref):
    total = own_ref[0]
    for place in range(32):
        total = total + arrived_ref[place].astype(f32)
    total = total.astype(bf16)
    for place in range(32):
        out_ref[place, 0:16, :] = total
        out_ref[place, 16:32, :] = second_ref[place]


def second_body(place_ref, arrived_ref, own_ref, between_ref, out_ref):
    batch, train = place_ref[0], place_ref[1]
    resid = unpack_from_train([arrived_ref[place, 0:16, :].astype(f32) for place in range(32)])
    change = dot_nn(resid.astype(bf16), between_ref[...]) * (-CUT * SCALE)
    total = own_ref[1]
    for place in range(32):
        total = total + arrived_ref[place, 16:32, :].astype(f32)
    mine = unpacked(total)
    group = lax.broadcasted_iota(jnp.int32, (ROWS, 256), 1) // 32
    change = change + jnp.where(group == batch, jnp.concatenate([mine] * 8, axis=1), 0.0)
    kept = unpacked(arrived_ref[train, 0:16, :].astype(f32))
    kept = jnp.concatenate([kept, jnp.zeros((ROWS, 96), f32)], axis=1)
    out = jnp.concatenate([change, kept], axis=1).astype(bf16)
    for place in range(8):
        out_ref[place] = out


def third_body(arrived_ref, library_ref, near_ref, out_ref, resid_ref):
    second = arrived_ref[0, :, 0:256].astype(f32)
    for place in range(1, 8):
        second = second + arrived_ref[place, :, 0:256].astype(f32)
    first = jnp.concatenate([arrived_ref[place, :, 256:288].astype(f32) for place in range(8)], axis=1)
    resid = jnp.concatenate([CUT * first, step_rate * second], axis=1)
    resid_ref[...] = jnp.concatenate([first, second], axis=1)
    total = library_ref[...] - SCALE * dot_nn(resid.astype(bf16), near_ref[...])
    pack_for_train(total, out_ref)


def update_body(resid_ref, local_ref, coef_ref, vel_ref, new_coef_ref, new_vel_ref):
    first, second = resid_ref[:, 0:256], resid_ref[:, 256:512]
    lanes = lax.broadcasted_iota(jnp.int32, (32, 4096), 1)
    spread = []
    for step in range(2):
        chosen = jnp.concatenate(
            [
                (lanes == local_ref[0:32, 8 * step + group : 8 * step + group + 1]).astype(bf16)
                for group in range(8)
            ],
            axis=0,
        )
        high, low = two_terms(first if step == 0 else second)
        spread.append(dot_nn(high, chosen) + dot_nn(low, chosen))
    grad_0, grad_1 = spread[0][0:33], spread[1][0:33]
    vel = momentum * vel_ref[...] - step_rate * grad_0
    coef = coef_ref[...] + vel
    vel = momentum * vel - step_rate * grad_1
    new_vel_ref[...] = vel
    new_coef_ref[...] = coef + vel


def final_body(arrived_ref, prior_ref, out_ref):
    total = arrived_ref[0].astype(f32)
    for place in range(1, 32):
        total = total + arrived_ref[place].astype(f32)
    shift = jnp.concatenate([jnp.zeros((1, 32), f32), prior_ref[...]], axis=0)
    out_ref[...] = unpacked(total)[0:33] + shift


def exchange(x, axis):
    return lax.all_to_all(x, axis, split_axis=0, concat_axis=0, tiled=True)


def per_device(
    batch_rows, train_embed, lib_embed, labels, prior_draws, noise_draws, coefficients, velocity, library_prior
):
    place = jnp.stack([lax.axis_index("batch"), lax.axis_index("train")]).astype(jnp.int32)
    rows = batch_rows
    block = shaped((32, 16, 128), bf16)
    cross = pltpu.VMEM((3, KEY_TILE, QUERY_TILE), f32)
    flops = 2 * 4096 * 1024 * 512
    picked = call(
        pick_body, shaped((2, 32, 256), bf16), place, rows, train_embed, name="pick", smem=1
    )

    def gathered(step):
        sent = jnp.broadcast_to(picked[step][None], (32, 32, 256))
        return exchange(sent, "train").reshape(1024, 256)

    queries_0 = gathered(0)
    queries_1 = gathered(1)
    ahead, base, own, picks, norms, same, local = call(
        prep_body,
        (
            shaped((ROWS, 4096), bf16), shaped((ROWS, 4096), bf16), shaped((2, 16, 128), f32),
            shaped((512, 256), bf16), shaped((4096, 1), f32), shaped((32, 256), f32),
            shaped((128, 16), jnp.int32),
        ),
        place, rows, train_embed, labels[None, :], prior_draws, noise_draws, coefficients, velocity,
        name="prep", smem=1, flops=flops // 2,
    )
    library, near = call(
        dense_library_body, (shaped((ROWS, 1024), f32), shaped((512, 1024), bf16)),
        train_embed, lib_embed, norms, base, picks,
        name="dense_library", scratch=(cross,), flops=flops,
    )
    total = pltpu.VMEM((ROWS, 1024), f32)
    part_0 = call(
        dense_batch_body, block, train_embed, queries_0, norms, ahead,
        name="dense_first", scratch=(cross, total), flops=flops,
    )
    arrived_0 = exchange(part_0, "train")
    part_1 = call(
        dense_batch_body, block, train_embed, queries_1, norms, base,
        name="dense_second", scratch=(cross, total), flops=flops,
    )
    between = call(
        between_body, shaped((1024, 256), bf16), place, queries_0, picks, same, name="between", smem=1, flops=flops // 16
    )
    sent_1 = call(first_body, shaped((32, 32, 128), bf16), arrived_0, own, part_1, name="first")
    arrived_1 = exchange(sent_1, "train")
    sent_2 = call(
        second_body, shaped((8, ROWS, 384), bf16), place, arrived_1, own, between, name="second", smem=1
    )
    arrived_2 = exchange(sent_2, "batch")
    sent_3, resid = call(
        third_body, (block, shaped((ROWS, 512), f32)), arrived_2, library, near, name="third"
    )
    arrived_3 = exchange(sent_3, "train")
    new_coef, new_vel = call(
        update_body, (shaped((33, 4096), f32), shaped((33, 4096), f32)), resid, local, coefficients, velocity,
        name="update",
    )
    predictions = call(final_body, shaped((33, 32), f32), arrived_3, library_prior, name="final")
    return new_coef, new_vel, predictions


def solution(mesh):
    return jax.shard_map(
        per_device,
        mesh=mesh,
        in_specs=(
            P(),
            P("train", None),
            P("batch", None),
            P("train"),
            P(None, "train"),
            P(None, "train"),
            P(None, "train"),
            P(None, "train"),
            P(None, ("batch", "train")),
        ),
        out_specs=(P(None, "train"), P(None, "train"), P(None, ("batch", "train"))),
        check_vma=False,
    )
```

```python
import jax
import jax.numpy as jnp
from jax import lax
from jax.experimental import pallas as pl
from jax.experimental.pallas import tpu as pltpu
from jax.sharding import PartitionSpec as P


momentum = 0.9
step_rate = 0.1
noise_var = 0.5
noise_scale = 0.7071067811865476
length_sq = 0.088

BETA = (5.0 / (length_sq * 256)) ** 0.5
SCALE = BETA * BETA / 3.0
C1 = 3.0 / BETA
C0 = 3.0 / (BETA * BETA)
RATE = BETA * 1.4426950408889634

CARRY = momentum + momentum * momentum
CUT = step_rate * (1.0 + momentum)

COLS = 33
HALF = 64
KEYS = 4096
QUERIES = 1024
TILE = 512
f32 = jnp.float32
bf16 = jnp.bfloat16

GRANT = 20 << 20


def call(body, ins, outs, scratch=(), flops=0):
    spec = {"H": pl.BlockSpec(memory_space=pltpu.HBM), "V": pl.BlockSpec(memory_space=pltpu.VMEM)}
    spec["P"] = spec["V"]
    spec["A"] = pl.BlockSpec(memory_space=pl.ANY)
    space = {"H": pltpu.HBM, "V": pltpu.VMEM, "P": pltpu.HBM, "A": pl.ANY}
    kernel = pl.pallas_call(
        body,
        out_shape=[space[kind](shape, dtype) for kind, shape, dtype in outs],
        in_specs=[spec[kind] for kind, _ in ins],
        out_specs=[spec[kind] for kind, _, _ in outs],
        scratch_shapes=list(scratch),
        compiler_params=pltpu.CompilerParams(vmem_limit_bytes=GRANT),
        cost_estimate=pl.CostEstimate(flops=flops, transcendentals=0, bytes_accessed=1 << 20),
    )
    result = kernel(*[pltpu.with_memory_space_constraint(array, space[kind]) for kind, array in ins])
    return result[0] if len(outs) == 1 else result


def places():
    return lax.axis_index("batch"), lax.axis_index("train")


def dot_nt(left, right):
    return lax.dot_general(left, right, (((1,), (1,)), ((), ())), preferred_element_type=f32)


def dot_nn(left, right):
    return jnp.dot(left, right, preferred_element_type=f32)


def two_terms(x):
    high = x.astype(bf16)
    return high, (x - high.astype(f32)).astype(bf16)


def norms_down(x):
    return jnp.sum(jnp.square(x.astype(f32)), axis=1, keepdims=True)


def norms_across(x):
    high, low = two_terms(jnp.square(x.astype(f32)))
    ones = jnp.ones((8, x.shape[1]), bf16)
    return (dot_nt(ones, high) + dot_nt(ones, low))[0:1]


def matern(cross, norms_q, norms_k):
    dist = jnp.maximum((norms_q + norms_k) + cross, 1e-12)
    root = dist * lax.rsqrt(dist)
    return ((root * (root + C1) + C0) * jnp.exp2(root * -RATE)).astype(bf16)


def local_rows(rows_ref, train, groups):
    chunks = []
    for step in range(2):
        for group in groups:
            start = group * QUERIES + (train // 4) * 128
            chunks.append(rows_ref[pl.ds(step, 1), pl.ds(pl.multiple_of(start, 128), 128)])
    while len(chunks) % 8:
        chunks.append(chunks[0])
    stack = jnp.concatenate(chunks, axis=0)
    stack = pltpu.roll(stack, lax.rem(128 - (train % 4) * 32, 128), axis=1)
    return stack - train * KEYS


def one_hot(column, start, width):
    lanes = lax.broadcasted_iota(jnp.int32, (column.shape[0], width), 1)
    return (lanes == column - start).astype(bf16)


def side_by_side(x):
    return jnp.concatenate([x[0:16], x[16:32]], axis=1)


def one_below_other(x):
    return jnp.concatenate([x[:, 0:HALF], x[:, HALF:]], axis=0)


def pack(total, out_ref):
    for place in range(32):
        out_ref[place] = side_by_side(total[32 * place : 32 * place + 32]).astype(bf16)


def pack_flipped(total, train, flips, out_ref):
    own = lax.rem(train, 4)
    for index, flip in enumerate(flips):
        other = lax.bitwise_xor(own, flip)
        for z in range(8):
            start = 256 * index + 32 * z
            out_ref[4 * z + other] = (SCALE * side_by_side(total[start : start + 32])).astype(bf16)


def pick_body(rows_hbm, embed_hbm, sent_hbm, rows, embed, picked, sems):
    batch, train = places()
    fetch = pltpu.make_async_copy(rows_hbm, rows, sems.at[0])
    fetch.start()
    chunks = []
    for index in range(4):
        part = pl.ds(1024 * index, 1024)
        chunks.append(pltpu.make_async_copy(embed_hbm.at[part], embed.at[part], sems.at[1 + index]))
        chunks[-1].start()
    fetch.wait()
    local = jnp.transpose(local_rows(rows, train, [batch]))
    column = jnp.concatenate([local[0:32, 0:1], local[0:32, 1:2]], axis=0)
    total = jnp.zeros((64, 256), f32)
    for index in range(4):
        chosen = one_hot(column, 1024 * index, 1024)
        chunks[index].wait()
        total = total + dot_nn(chosen, embed[1024 * index : 1024 * index + 1024, :])
    picked[0] = total[0:32].astype(bf16)
    picked[1] = total[32:64].astype(bf16)
    out = [pltpu.make_async_copy(picked, sent_hbm.at[z], sems.at[5 + z]) for z in range(8)]
    for copy in out:
        copy.start()
    for copy in out:
        copy.wait()


def prep_body(
    rows_ref, embed_hbm, labels_hbm, prior_hbm, noise_hbm, coef_hbm, vel_hbm,
    ahead_hbm, base_hbm, own_ref, norms_ref,
    embed, labels, prior, noise, coef, vel, ahead_half, base_half, sems,
):
    batch, train = places()
    copies = [
        pltpu.make_async_copy(source, target, sems.at[index])
        for index, (source, target) in enumerate(
            [
                (coef_hbm, coef), (vel_hbm, vel), (prior_hbm, prior), (noise_hbm, noise), (labels_hbm, labels),
                (embed_hbm, embed),
            ]
        )
    ]
    for copy in copies:
        copy.start()
    mine = jnp.transpose(local_rows(rows_ref, train, [batch]))
    for copy in copies[:2]:
        copy.wait()
    ahead = coef[...] + momentum * vel[...]
    base = coef[...] + CARRY * vel[...]
    pad = jnp.zeros((HALF - COLS, KEYS), f32)
    ahead_half[...] = jnp.concatenate([ahead, pad], axis=0).astype(bf16)
    base_half[...] = jnp.concatenate([base, pad], axis=0).astype(bf16)
    out = [
        pltpu.make_async_copy(ahead_half, ahead_hbm, sems.at[6]),
        pltpu.make_async_copy(base_half, base_hbm, sems.at[7]),
    ]
    for copy in out:
        copy.start()
    for copy in copies[2:]:
        copy.wait()
    shift = jnp.concatenate([jnp.zeros((1, KEYS), f32), prior[...] + noise_scale * noise[...]], axis=0)
    targets = labels[...] - shift
    for step, state in enumerate((ahead, base)):
        chosen = one_hot(mine[0:32, step : step + 1], 0, KEYS)
        high, low = two_terms(jnp.concatenate([noise_var * state - targets, pad], axis=0))
        own_ref[step] = side_by_side(dot_nt(chosen, high) + dot_nt(chosen, low))
    norms_ref[...] = norms_across(embed[...])
    for copy in out:
        copy.wait()


def dense_scratch(queries):
    return [
        pltpu.VMEM((KEYS, 256), bf16),
        pltpu.VMEM((queries, 256), bf16),
        pltpu.VMEM((HALF, KEYS), bf16),
        pltpu.VMEM((queries, 1), f32),
        pltpu.VMEM((2, queries, TILE), f32),
        pltpu.VMEM((queries, HALF), f32),
        pltpu.SemaphoreType.DMA((13,)),
    ]


def dense(embed_hbm, pieces, weight_hbm, norms_ref, scratch, tiles, start_ref=None, short=False):
    embed, query, weight, query_norms, cross, total_ref, sems = scratch
    first, count = tiles

    def chunk(index):
        part = pl.ds(pl.multiple_of((first + index) * TILE, TILE), TILE)
        return pltpu.make_async_copy(embed_hbm.at[part], embed.at[part], sems.at[index])

    rows = query.shape[0] // len(pieces)
    fetches = [
        pltpu.make_async_copy(piece, query.at[pl.ds(rows * index, rows)], sems.at[9 + index])
        for index, piece in enumerate(pieces)
    ]
    fetch_weight = pltpu.make_async_copy(weight_hbm, weight, sems.at[8])
    for fetch in fetches:
        fetch.start()
    chunk(0).start()
    fetch_weight.start()
    for index in range(1, count):
        chunk(index).start()
    total_ref[...] = jnp.zeros_like(total_ref) if start_ref is None else start_ref[...]
    for index, fetch in enumerate(fetches):
        fetch.wait()
        part = slice(rows * index, rows * index + rows)
        query_norms[part, :] = norms_down(query[part, :])
        query[part, :] = query[part, :] * bf16(-2)

    def keys(index):
        return pl.ds(pl.multiple_of((first + index) * TILE, TILE), TILE)

    def product(index):
        return dot_nt(query[...], embed[keys(index), :])

    chunk(0).wait()
    cross[0] = product(0)
    fetch_weight.wait()

    def one(index, slot, more):
        if more:
            cross[1 - slot] = product(jnp.minimum(index + 1, count - 1) if short else index + 1)
        value = matern(cross[slot], query_norms[...], norms_ref[:, keys(index)])
        total_ref[...] += dot_nt(value, weight[:, keys(index)])

    def pair(index, carry):
        chunk(2 * index + 1).wait()
        if short:

            @pl.when(2 * index + 2 < count)
            def _():
                chunk(2 * index + 2).wait()

            one(2 * index, 0, True)
            one(2 * index + 1, 1, True)
        else:
            chunk(2 * index + 2).wait()
            one(2 * index, 0, True)
            one(2 * index + 1, 1, True)
        return carry

    if short:
        lax.fori_loop(0, count // 2, pair, 0)
        return total_ref
    loops = (count - 1) // 2
    lax.fori_loop(0, loops, pair, 0)
    for index in range(2 * loops, count):
        more = index + 1 < count
        if more:
            chunk(index + 1).wait()
        one(index, index % 2, more)
    return total_ref


def dense_first_body(embed, own, flip, weight, norms_ref, after, out_ref, *scratch):
    del after
    total = dense(embed, [own, flip], weight, norms_ref, scratch, (0, 8))
    for index in range(16):
        out_ref[index] = (SCALE * side_by_side(total[32 * index : 32 * index + 32])).astype(bf16)


def dense_rest_body(embed, flip_2, flip_3, weight, norms_ref, done_ref, out_ref, *scratch):
    train = places()[1]
    total = dense(embed, [flip_2, flip_3], weight, norms_ref, scratch, (0, 8))
    pack_flipped(total, train, (2, 3), out_ref)
    own = lax.rem(train, 4)
    for index in range(2):
        other = lax.bitwise_xor(own, index)
        for z in range(8):
            out_ref[4 * z + other] = done_ref[8 * index + z]


def dense_second_body(embed, flip_0, flip_1, flip_2, flip_3, weight, norms_ref, after, out_ref, *scratch):
    del after
    total = dense(embed, [flip_0, flip_1, flip_2, flip_3], weight, norms_ref, scratch, (0, 8))
    pack_flipped(total, places()[1], range(4), out_ref)


LIBRARY_SPLIT = 4


def library_first_body(embed, query, weight, norms_ref, after, out_ref, *scratch):
    del after
    total = dense(embed, [query], weight, norms_ref, scratch, (0, LIBRARY_SPLIT), short=True)
    out_ref[...] = total[...]


def library_second_body(embed, query, weight, norms_ref, start_ref, after, out_ref, *scratch):
    del after
    total = dense(embed, [query], weight, norms_ref, scratch, (LIBRARY_SPLIT, 8 - LIBRARY_SPLIT), start_ref, True)
    out_ref[...] = total[...]


def near_body(rows_ref, embed_hbm, library_hbm, after, near, picks, local_ref, embed, library, sems):
    del after
    copies = [
        pltpu.make_async_copy(embed_hbm, embed, sems.at[0]),
        pltpu.make_async_copy(library_hbm, library, sems.at[1]),
    ]
    for copy in copies:
        copy.start()
    train = places()[1]
    local = jnp.transpose(local_rows(rows_ref, train, range(8)))
    local_ref[...] = local
    column = jnp.concatenate([local[0:32, index : index + 1] for index in range(16)], axis=0)
    for copy in copies:
        copy.wait()
    for index in range(4):
        part = slice(128 * index, 128 * index + 128)
        picks[part, :] = dot_nn(one_hot(column[part], 0, KEYS), embed[...]).astype(bf16)
    pick_norms = norms_across(picks[...])
    for index in range(2):
        part = slice(512 * index, 512 * index + 512)
        queries = library[part, :]
        near[part, :] = matern(dot_nt(queries * bf16(-2), picks[...]), norms_down(queries), pick_norms)


def between_body(rows_ref, flip_0, flip_1, flip_2, flip_3, picks, local_ref, after, between, query, sems):
    del after
    copies = []
    for index, flip in enumerate((flip_0, flip_1, flip_2, flip_3)):
        copies.append(pltpu.make_async_copy(flip, query.at[index], sems.at[index]))
        copies[-1].start()
    batch, train = places()
    column = jnp.concatenate([local_ref[0:32, index : index + 1] for index in range(8, 16)], axis=0)
    mine = local_rows(rows_ref, train, [batch])[0:1, 0:32]
    mine = jnp.concatenate([mine] * 8, axis=1)
    z = lax.broadcasted_iota(jnp.int32, (256, 256), 1) // 32
    same = jnp.where((column == mine) & (z == train // 4), noise_var / SCALE, 0.0)
    second = picks[256:512, :]
    second_norms = norms_down(second)
    second = second * bf16(-2)
    for index, copy in enumerate(copies):
        copy.wait()
        value = matern(dot_nt(second, query[index]), second_norms, norms_across(query[index]))
        if index == 0:
            value = (value.astype(f32) + same).astype(bf16)
        between[:, 256 * index : 256 * index + 256] = value


def first_body(arrived_ref, own_ref, second_ref, out_ref):
    total = own_ref[0]
    for place in range(32):
        total = total + arrived_ref[place].astype(f32)
    total = total.astype(bf16)
    for place in range(32):
        out_ref[place, 0:16, :] = total
        out_ref[place, 16:32, :] = second_ref[place]


def second_body(arrived_ref, own_ref, between, after, out_ref, resid):
    del after
    batch, train = places()
    total = own_ref[1]
    for place in range(32):
        total = total + arrived_ref[place, 16:32, :].astype(f32)
    own = lax.rem(train, 4)
    for flip in range(4):
        other = lax.bitwise_xor(own, flip)
        for z in range(8):
            start = 256 * flip + 32 * z
            resid[start : start + 32, :] = one_below_other(arrived_ref[4 * z + other, 0:16, :])
    mine = one_below_other(total)
    change = dot_nn(between[...], resid[...]) * (-CUT * SCALE)
    group = lax.broadcasted_iota(jnp.int32, (256, HALF), 0) // 32
    change = change + jnp.where(group == batch, jnp.concatenate([mine] * 8, axis=0), 0.0)
    change = jnp.concatenate([change[0:128], change[128:256]], axis=1).astype(bf16)
    kept = arrived_ref[train, 0:16, :]
    for place in range(8):
        out_ref[place, 0:128, :] = change
        out_ref[place, 128:144, :] = kept


def third_body(arrived_ref, library, near, out_ref, resid_ref):
    second = arrived_ref[0, 0:128, :].astype(f32)
    for place in range(1, 8):
        second = second + arrived_ref[place, 0:128, :].astype(f32)
    second = jnp.concatenate([second[:, 0:HALF], second[:, HALF:]], axis=0)
    first = jnp.concatenate([one_below_other(arrived_ref[place, 128:144, :].astype(f32)) for place in range(8)], axis=0)
    resid_ref[...] = jnp.concatenate([first, second], axis=0)
    resid = jnp.concatenate([CUT * first, step_rate * second], axis=0).astype(bf16)
    total = SCALE * (library[...] - dot_nn(near[...], resid))
    pack(total, out_ref)


def update_body(resid_ref, local_ref, coef_ref, vel_ref, new_coef_ref, new_vel_ref):
    lanes = jnp.concatenate([resid_ref[...], jnp.zeros((512, 128 - HALF), f32)], axis=1)
    across = jnp.transpose(lanes)[0:48]
    grads = []
    for step in range(2):
        column = jnp.concatenate(
            [local_ref[0:32, 8 * step + group : 8 * step + group + 1] for group in range(8)], axis=0
        )
        high, low = two_terms(across[:, 256 * step : 256 * step + 256])
        chosen = one_hot(column, 0, KEYS)
        grads.append((dot_nn(high, chosen) + dot_nn(low, chosen))[0:COLS])
    vel = momentum * vel_ref[...] - step_rate * grads[0]
    coef = coef_ref[...] + vel
    vel = momentum * vel - step_rate * grads[1]
    new_vel_ref[...] = vel
    new_coef_ref[...] = coef + vel


def final_body(arrived_ref, prior_ref, out_ref):
    total = arrived_ref[0].astype(f32)
    for place in range(1, 32):
        total = total + arrived_ref[place].astype(f32)
    total = one_below_other(total)[:, 0:COLS]
    out_ref[...] = total + jnp.concatenate([jnp.zeros((32, 1), f32), jnp.transpose(prior_ref[...])], axis=1)


def exchange(x, axis):
    return lax.all_to_all(x, axis, split_axis=0, concat_axis=0, tiled=True)


def whole(
    batch_rows, train_embed, lib_embed, labels, prior_draws, noise_draws, coefficients, velocity, library_prior
):
    flops = 2 * KEYS * QUERIES * 512
    dma = pltpu.SemaphoreType.DMA
    vmem = pltpu.VMEM
    block = ("P", (32, 16, 128), bf16)
    sent, rows = call(
        pick_body, [("H", batch_rows), ("H", train_embed)],
        [("H", (8, 2, 32, 256), bf16), ("V", (2, 8192), jnp.int32)],
        [vmem((KEYS, 256), bf16), vmem((2, 32, 256), bf16), dma((13,))],
    )
    columns = [[4 * z + chip for z in range(8)] for chip in range(4)]
    column = lax.all_to_all(sent, "train", 0, 0, axis_index_groups=columns, tiled=True)
    flips = []
    for step in range(2):
        own_part = column[:, step].reshape(256, 256)
        flips.append([own_part])
        for flip in range(1, 4):
            flips[step].append(lax.ppermute(own_part, "train", [(t, t ^ flip) for t in range(32)]))
    state = vmem((COLS, KEYS), f32)
    draws = vmem((COLS - 1, KEYS), f32)
    half = vmem((HALF, KEYS), bf16)
    ahead, base, own, norms = call(
        prep_body,
        [
            ("V", rows), ("H", train_embed), ("H", labels[None, :]), ("H", prior_draws),
            ("H", noise_draws), ("H", coefficients), ("H", velocity),
        ],
        [
            ("H", (HALF, KEYS), bf16), ("H", (HALF, KEYS), bf16), ("V", (2, 16, 128), f32), ("V", (1, KEYS), f32),
        ],
        [vmem((KEYS, 256), bf16), vmem((1, KEYS), f32), draws, draws, state, state, half, half, dma((8,))],
        flops // 4,
    )
    near, picks, local = call(
        near_body,
        [("V", rows), ("H", train_embed), ("H", lib_embed), ("H", base)],
        [("V", (QUERIES, 512), bf16), ("V", (512, 256), bf16), ("V", (128, 16), jnp.int32)],
        [vmem((KEYS, 256), bf16), vmem((QUERIES, 256), bf16), dma((2,))], flops // 4,
    )
    library_part = call(
        library_first_body,
        [("H", train_embed), ("H", lib_embed), ("H", base), ("V", norms), ("V", near)],
        [("V", (QUERIES, HALF), f32)], dense_scratch(QUERIES), flops * LIBRARY_SPLIT // 8,
    )
    part_half = call(
        dense_first_body,
        [("H", train_embed), ("A", flips[0][0]), ("A", flips[0][1]), ("H", ahead), ("V", norms), ("V", library_part)],
        [("V", (16, 16, 128), bf16)], dense_scratch(512), flops // 2,
    )
    part_0 = call(
        dense_rest_body,
        [("H", train_embed), ("A", flips[0][2]), ("A", flips[0][3]), ("H", ahead), ("V", norms), ("V", part_half)],
        [block], dense_scratch(512), flops // 2,
    )
    arrived_0 = exchange(part_0, "train")
    part_1 = call(
        dense_second_body,
        [("H", train_embed), *[("A", part) for part in flips[1]], ("H", base), ("V", norms), ("H", part_0)],
        [("V", (32, 16, 128), bf16)], dense_scratch(QUERIES), flops,
    )
    sent_1 = call(first_body, [("V", arrived_0), ("V", own), ("V", part_1)], [("P", (32, 32, 128), bf16)])
    arrived_1 = exchange(sent_1, "train")
    between = call(
        between_body,
        [("V", rows), *[("A", part) for part in flips[0]], ("V", picks), ("V", local), ("H", sent_1)],
        [("V", (256, QUERIES), bf16)], [vmem((4, 256, 256), bf16), dma((4,))], flops // 16,
    )
    library = call(
        library_second_body,
        [("H", train_embed), ("H", lib_embed), ("H", base), ("V", norms), ("V", library_part), ("V", between)],
        [("V", (QUERIES, HALF), f32)], dense_scratch(QUERIES), flops * (8 - LIBRARY_SPLIT) // 8,
    )
    sent_2 = call(
        second_body, [("V", arrived_1), ("V", own), ("V", between), ("V", library)],
        [("V", (8, 144, 128), bf16)], [vmem((QUERIES, HALF), bf16)],
    )
    arrived_2 = exchange(sent_2, "batch")
    sent_3, resid = call(third_body, [("V", arrived_2), ("V", library), ("V", near)], [block, ("V", (512, HALF), f32)])
    arrived_3 = exchange(sent_3, "train")
    new_coef, new_vel = call(
        update_body, [("V", resid), ("V", local), ("V", coefficients), ("V", velocity)],
        [("P", (COLS, KEYS), f32), ("P", (COLS, KEYS), f32)],
    )
    predictions = call(final_body, [("V", arrived_3), ("V", library_prior)], [("P", (32, COLS), f32)])
    return new_coef, new_vel, predictions.T


def solution(mesh):
    return jax.shard_map(
        whole,
        mesh=mesh,
        in_specs=(
            P(),
            P("train", None),
            P("batch", None),
            P("train"),
            P(None, "train"),
            P(None, "train"),
            P(None, "train"),
            P(None, "train"),
            P(None, ("batch", "train")),
        ),
        out_specs=(P(None, "train"), P(None, "train"), P(None, ("batch", "train"))),
        check_vma=False,
    )
```

```python
import jax
import jax.numpy as jnp
from jax import lax
from jax.experimental import pallas as pl
from jax.experimental.pallas import tpu as pltpu
from jax.sharding import PartitionSpec as P


momentum = 0.9
step_rate = 0.1
noise_var = 0.5
noise_scale = 0.7071067811865476
length_sq = 0.088

BETA = (5.0 / (length_sq * 256)) ** 0.5
SCALE = BETA * BETA / 3.0
C1 = 3.0 / BETA
C0 = 3.0 / (BETA * BETA)
RATE = BETA * 1.4426950408889634

CARRY = momentum + momentum * momentum
CUT = step_rate * (1.0 + momentum)

COLS = 33
HALF = 64
KEYS = 4096
QUERIES = 1024
TILE = 512
f32 = jnp.float32
bf16 = jnp.bfloat16

GRANT = 20 << 20


def call(body, ins, outs, scratch=(), flops=0):
    spec = {"H": pl.BlockSpec(memory_space=pltpu.HBM), "V": pl.BlockSpec(memory_space=pltpu.VMEM)}
    spec["P"] = spec["V"]
    spec["A"] = pl.BlockSpec(memory_space=pl.ANY)
    space = {"H": pltpu.HBM, "V": pltpu.VMEM, "P": pltpu.HBM, "A": pl.ANY}
    kernel = pl.pallas_call(
        body,
        out_shape=[space[kind](shape, dtype) for kind, shape, dtype in outs],
        in_specs=[spec[kind] for kind, _ in ins],
        out_specs=[spec[kind] for kind, _, _ in outs],
        scratch_shapes=list(scratch),
        compiler_params=pltpu.CompilerParams(vmem_limit_bytes=GRANT),
        cost_estimate=pl.CostEstimate(flops=flops, transcendentals=0, bytes_accessed=1 << 20),
    )
    result = kernel(*[pltpu.with_memory_space_constraint(array, space[kind]) for kind, array in ins])
    return result[0] if len(outs) == 1 else result


def places():
    return lax.axis_index("batch"), lax.axis_index("train")


def dot_nt(left, right):
    return lax.dot_general(left, right, (((1,), (1,)), ((), ())), preferred_element_type=f32)


def dot_nn(left, right):
    return jnp.dot(left, right, preferred_element_type=f32)


def two_terms(x):
    high = x.astype(bf16)
    return high, (x - high.astype(f32)).astype(bf16)


def norms_down(x):
    return jnp.sum(jnp.square(x.astype(f32)), axis=1, keepdims=True)


def norms_across(x):
    high, low = two_terms(jnp.square(x.astype(f32)))
    ones = jnp.ones((8, x.shape[1]), bf16)
    return (dot_nt(ones, high) + dot_nt(ones, low))[0:1]


def matern(cross, norms_q, norms_k):
    dist = jnp.maximum((norms_q + norms_k) + cross, 1e-12)
    root = dist * lax.rsqrt(dist)
    return ((root * (root + C1) + C0) * jnp.exp2(root * -RATE)).astype(bf16)


def local_rows(rows_ref, train, groups):
    chunks = []
    for step in range(2):
        for group in groups:
            start = group * QUERIES + (train // 4) * 128
            chunks.append(rows_ref[pl.ds(step, 1), pl.ds(pl.multiple_of(start, 128), 128)])
    while len(chunks) % 8:
        chunks.append(chunks[0])
    stack = jnp.concatenate(chunks, axis=0)
    stack = pltpu.roll(stack, lax.rem(128 - (train % 4) * 32, 128), axis=1)
    return stack - train * KEYS


def one_hot(column, start, width):
    lanes = lax.broadcasted_iota(jnp.int32, (column.shape[0], width), 1)
    return (lanes == column - start).astype(bf16)


def side_by_side(x):
    return jnp.concatenate([x[0:16], x[16:32]], axis=1)


def one_below_other(x):
    return jnp.concatenate([x[:, 0:HALF], x[:, HALF:]], axis=0)


def pack(total, out_ref):
    for place in range(32):
        out_ref[place] = side_by_side(total[32 * place : 32 * place + 32]).astype(bf16)


def pack_flipped(total, train, flips, out_ref):
    own = lax.rem(train, 4)
    for index, flip in enumerate(flips):
        other = lax.bitwise_xor(own, flip)
        for z in range(8):
            start = 256 * index + 32 * z
            out_ref[4 * z + other] = (SCALE * side_by_side(total[start : start + 32, 0:HALF])).astype(bf16)


def pick_body(rows_hbm, embed_hbm, sent_hbm, rows, embed, picked, sems):
    batch, train = places()
    fetch = pltpu.make_async_copy(rows_hbm, rows, sems.at[0])
    fetch.start()
    chunks = []
    for index in range(4):
        part = pl.ds(1024 * index, 1024)
        chunks.append(pltpu.make_async_copy(embed_hbm.at[part], embed.at[part], sems.at[1 + index]))
        chunks[-1].start()
    fetch.wait()
    local = jnp.transpose(local_rows(rows, train, [batch]))
    column = jnp.concatenate([local[0:32, 0:1], local[0:32, 1:2]], axis=0)
    total = jnp.zeros((64, 256), f32)
    for index in range(4):
        chosen = one_hot(column, 1024 * index, 1024)
        chunks[index].wait()
        total = total + dot_nn(chosen, embed[1024 * index : 1024 * index + 1024, :])
    picked[0] = total[0:32].astype(bf16)
    picked[1] = total[32:64].astype(bf16)
    out = [pltpu.make_async_copy(picked, sent_hbm.at[z], sems.at[5 + z]) for z in range(8)]
    for copy in out:
        copy.start()
    for copy in out:
        copy.wait()


def turned(state):
    full = jnp.concatenate([state, jnp.zeros((40 - COLS, KEYS), f32)], axis=0)
    rest = jnp.zeros((128, 128 - 40), f32)
    return [
        jnp.concatenate([jnp.transpose(full[:, 128 * index : 128 * index + 128]), rest], axis=1).astype(bf16)
        for index in range(KEYS // 128)
    ]


def prep_body(
    rows_ref, embed_hbm, library_hbm, labels_hbm, prior_hbm, noise_hbm, coef_hbm, vel_hbm,
    ahead_hbm, base_hbm, own_ref, norms_ref, picks, local_ref, part_hbm,
    labels, prior, noise, coef, vel, ahead_half, sems, *scratch,
):
    embed, query, base_half, query_norms, cross, total, _ = scratch
    batch, train = places()
    copies = [
        pltpu.make_async_copy(source, target, sems.at[index])
        for index, (source, target) in enumerate(
            [
                (coef_hbm, coef), (vel_hbm, vel), (prior_hbm, prior), (noise_hbm, noise), (labels_hbm, labels),
                (embed_hbm, embed), (library_hbm, query),
            ]
        )
    ]
    for copy in copies:
        copy.start()
    mine = jnp.transpose(local_rows(rows_ref, train, [batch]))
    local = jnp.transpose(local_rows(rows_ref, train, range(8)))
    local_ref[...] = local
    for copy in copies[:2]:
        copy.wait()
    ahead = coef[...] + momentum * vel[...]
    base = coef[...] + CARRY * vel[...]
    for index, (one, two) in enumerate(zip(turned(ahead), turned(base))):
        ahead_half[128 * index : 128 * index + 128, :] = one
        base_half[128 * index : 128 * index + 128, :] = two
    out = [
        pltpu.make_async_copy(ahead_half, ahead_hbm, sems.at[7]),
        pltpu.make_async_copy(base_half, base_hbm, sems.at[8]),
    ]
    for copy in out:
        copy.start()
    for copy in copies[2:]:
        copy.wait()
    shift = jnp.concatenate([jnp.zeros((1, KEYS), f32), prior[...] + noise_scale * noise[...]], axis=0)
    targets = labels[...] - shift
    pad = jnp.zeros((HALF - COLS, KEYS), f32)
    for step, state in enumerate((ahead, base)):
        chosen = one_hot(mine[0:32, step : step + 1], 0, KEYS)
        high, low = two_terms(jnp.concatenate([noise_var * state - targets, pad], axis=0))
        own_ref[step] = side_by_side(dot_nt(chosen, high) + dot_nt(chosen, low))
    norms_ref[...] = norms_across(embed[...])
    column = jnp.concatenate([local[0:32, index : index + 1] for index in range(16)], axis=0)
    for index in range(4):
        part = slice(128 * index, 128 * index + 128)
        picks[part, :] = dot_nn(one_hot(column[part], 0, KEYS), embed[...]).astype(bf16)
    total[...] = jnp.zeros_like(total)
    scaled(query, query_norms, slice(0, QUERIES))
    sweep(embed, query, base_half, query_norms, cross, total, norms_ref, (0, LIBRARY_SPLIT), None, True)
    out.append(pltpu.make_async_copy(total, part_hbm, sems.at[9]))
    out[-1].start()
    for copy in out:
        copy.wait()


LIBRARY_SPLIT = 4


def scaled(query, query_norms, part):
    query_norms[part, :] = norms_down(query[part, :])
    query[part, :] = query[part, :] * bf16(-2)


def sweep(embed, query, weight, query_norms, cross, total, norms_ref, tiles, wait, short):
    first, count = tiles

    def keys(index):
        return pl.ds(pl.multiple_of((first + index) * TILE, TILE), TILE)

    def product(index):
        return dot_nt(query[...], embed[keys(index), :])

    def one(index, slot, more):
        if more:
            cross[1 - slot] = product(jnp.minimum(index + 1, count - 1) if short else index + 1)
        value = matern(cross[slot], query_norms[...], norms_ref[:, keys(index)])
        total[...] += dot_nn(value, weight[keys(index), :])

    if wait is not None:
        wait(0)
    cross[0] = product(0)

    def pair(index, carry):
        if wait is not None:
            wait(2 * index + 1)
            if short:
                pl.when(2 * index + 2 < count)(lambda: wait(2 * index + 2))
            else:
                wait(2 * index + 2)
        one(2 * index, 0, True)
        one(2 * index + 1, 1, True)
        return carry

    loops = count // 2 if short else (count - 1) // 2
    lax.fori_loop(0, loops, pair, 0)
    for index in range(2 * loops, count):
        more = index + 1 < count
        if more and wait is not None:
            wait(index + 1)
        one(index, index % 2, more)


def dense_scratch(queries):
    return [
        pltpu.VMEM((KEYS, 256), bf16),
        pltpu.VMEM((queries, 256), bf16),
        pltpu.VMEM((KEYS, 128), bf16),
        pltpu.VMEM((queries, 1), f32),
        pltpu.VMEM((2, queries, TILE), f32),
        pltpu.VMEM((queries, 128), f32),
        pltpu.SemaphoreType.DMA((20,)),
    ]


def dense(embed_hbm, pieces, weight_hbm, norms_ref, scratch, tiles, start_hbm=None, between=None, short=False):
    embed, query, weight, query_norms, cross, total, sems = scratch
    first, count = tiles

    def chunk(index):
        part = pl.ds(pl.multiple_of((first + index) * TILE, TILE), TILE)
        return (
            pltpu.make_async_copy(embed_hbm.at[part], embed.at[part], sems.at[index]),
            pltpu.make_async_copy(weight_hbm.at[part], weight.at[part], sems.at[8 + index]),
        )

    def wait(index):
        for copy in chunk(index):
            copy.wait()

    rows = query.shape[0] // len(pieces)
    fetches = [
        pltpu.make_async_copy(piece, query.at[pl.ds(rows * index, rows)], sems.at[16 + index])
        for index, piece in enumerate(pieces)
    ]
    for fetch in fetches:
        fetch.start()
    for index in range(count):
        for copy in chunk(index):
            copy.start()
    if start_hbm is None:
        total[...] = jnp.zeros_like(total)
    else:
        fetch_start = pltpu.make_async_copy(start_hbm, total, sems.at[17])
        fetch_start.start()
    if between is not None:
        between()
    for index, fetch in enumerate(fetches):
        fetch.wait()
        scaled(query, query_norms, slice(rows * index, rows * index + rows))
    if start_hbm is not None:
        fetch_start.wait()
    sweep(embed, query, weight, query_norms, cross, total, norms_ref, tiles, wait, short)
    return total


def dense_first_body(embed, own, flip, weight, norms_ref, out_ref, *scratch):
    total = dense(embed, [own, flip], weight, norms_ref, scratch, (0, 8))
    for index in range(16):
        out_ref[index] = (SCALE * side_by_side(total[32 * index : 32 * index + 32, 0:HALF])).astype(bf16)


def dense_rest_body(embed, flip_2, flip_3, weight, norms_ref, done_ref, out_ref, *scratch):
    train = places()[1]
    total = dense(embed, [flip_2, flip_3], weight, norms_ref, scratch, (0, 8))
    pack_flipped(total, train, (2, 3), out_ref)
    own = lax.rem(train, 4)
    for index in range(2):
        other = lax.bitwise_xor(own, index)
        for z in range(8):
            out_ref[4 * z + other] = done_ref[8 * index + z]


def dense_second_body(embed, flip_0, flip_1, flip_2, flip_3, weight, norms_ref, after, out_ref, *scratch):
    del after
    total = dense(embed, [flip_0, flip_1, flip_2, flip_3], weight, norms_ref, scratch, (0, 8))
    pack_flipped(total, places()[1], range(4), out_ref)


def between_body(
    rows_ref, flip_0, flip_1, flip_2, flip_3, picks, local_ref, embed_hbm, library_hbm, weight_hbm, norms_ref, start_hbm,
    after, between, out_ref, first, sems, *scratch,
):
    del after
    copies = []
    for index, flip in enumerate((flip_0, flip_1, flip_2, flip_3)):
        copies.append(pltpu.make_async_copy(flip, first.at[index], sems.at[index]))
        copies[-1].start()

    def tile():
        batch, train = places()
        column = jnp.concatenate([local_ref[0:32, index : index + 1] for index in range(8, 16)], axis=0)
        mine = local_rows(rows_ref, train, [batch])[0:1, 0:32]
        mine = jnp.concatenate([mine] * 8, axis=1)
        z = lax.broadcasted_iota(jnp.int32, (256, 256), 1) // 32
        same = jnp.where((column == mine) & (z == train // 4), noise_var / SCALE, 0.0)
        second = picks[256:512, :]
        second_norms = norms_down(second)
        second = second * bf16(-2)
        for index, copy in enumerate(copies):
            copy.wait()
            value = matern(dot_nt(second, first[index]), second_norms, norms_across(first[index]))
            if index == 0:
                value = (value.astype(f32) + same).astype(bf16)
            between[:, 256 * index : 256 * index + 256] = value

    tiles = (LIBRARY_SPLIT, 8 - LIBRARY_SPLIT)
    total = dense(embed_hbm, [library_hbm], weight_hbm, norms_ref, scratch, tiles, start_hbm, tile, True)
    out_ref[...] = total[...]


def near_body(library_hbm, picks, after, near, library, sem):
    del after
    copy = pltpu.make_async_copy(library_hbm, library, sem)
    copy.start()
    pick_norms = norms_across(picks[...])
    copy.wait()
    for index in range(2):
        part = slice(512 * index, 512 * index + 512)
        queries = library[part, :]
        near[part, :] = matern(dot_nt(queries * bf16(-2), picks[...]), norms_down(queries), pick_norms)


def first_body(arrived_ref, own_ref, second_ref, out_ref):
    total = own_ref[0]
    for place in range(32):
        total = total + arrived_ref[place].astype(f32)
    total = total.astype(bf16)
    for place in range(32):
        out_ref[place, 0:16, :] = total
        out_ref[place, 16:32, :] = second_ref[place]


def second_body(arrived_ref, own_ref, between, out_ref, resid):
    batch, train = places()
    total = own_ref[1]
    for place in range(32):
        total = total + arrived_ref[place, 16:32, :].astype(f32)
    own = lax.rem(train, 4)
    for flip in range(4):
        other = lax.bitwise_xor(own, flip)
        for z in range(8):
            start = 256 * flip + 32 * z
            resid[start : start + 32, :] = one_below_other(arrived_ref[4 * z + other, 0:16, :])
    mine = one_below_other(total)
    change = dot_nn(between[...], resid[...]) * (-CUT * SCALE)
    group = lax.broadcasted_iota(jnp.int32, (256, HALF), 0) // 32
    change = change + jnp.where(group == batch, jnp.concatenate([mine] * 8, axis=0), 0.0)
    change = jnp.concatenate([change[0:128], change[128:256]], axis=1).astype(bf16)
    kept = arrived_ref[train, 0:16, :]
    for place in range(8):
        out_ref[place, 0:128, :] = change
        out_ref[place, 128:144, :] = kept


def third_body(arrived_ref, library, near, out_ref, resid_ref):
    second = arrived_ref[0, 0:128, :].astype(f32)
    for place in range(1, 8):
        second = second + arrived_ref[place, 0:128, :].astype(f32)
    second = jnp.concatenate([second[:, 0:HALF], second[:, HALF:]], axis=0)
    first = jnp.concatenate([one_below_other(arrived_ref[place, 128:144, :].astype(f32)) for place in range(8)], axis=0)
    resid_ref[...] = jnp.concatenate([first, second], axis=0)
    resid = jnp.concatenate([CUT * first, step_rate * second], axis=0).astype(bf16)
    total = SCALE * (library[:, 0:HALF] - dot_nn(near[...], resid))
    pack(total, out_ref)


def update_body(resid_ref, local_ref, coef_ref, vel_ref, new_coef_ref, new_vel_ref):
    lanes = jnp.concatenate([resid_ref[...], jnp.zeros((512, 128 - HALF), f32)], axis=1)
    across = jnp.transpose(lanes)[0:48]
    grads = []
    for step in range(2):
        column = jnp.concatenate(
            [local_ref[0:32, 8 * step + group : 8 * step + group + 1] for group in range(8)], axis=0
        )
        high, low = two_terms(across[:, 256 * step : 256 * step + 256])
        chosen = one_hot(column, 0, KEYS)
        grads.append((dot_nn(high, chosen) + dot_nn(low, chosen))[0:COLS])
    vel = momentum * vel_ref[...] - step_rate * grads[0]
    coef = coef_ref[...] + vel
    vel = momentum * vel - step_rate * grads[1]
    new_vel_ref[...] = vel
    new_coef_ref[...] = coef + vel


def final_body(arrived_ref, prior_ref, out_ref):
    total = arrived_ref[0].astype(f32)
    for place in range(1, 32):
        total = total + arrived_ref[place].astype(f32)
    total = one_below_other(total)[:, 0:COLS]
    out_ref[...] = total + jnp.concatenate([jnp.zeros((32, 1), f32), jnp.transpose(prior_ref[...])], axis=1)


def exchange(x, axis):
    return lax.all_to_all(x, axis, split_axis=0, concat_axis=0, tiled=True)


def whole(
    batch_rows, train_embed, lib_embed, labels, prior_draws, noise_draws, coefficients, velocity, library_prior
):
    flops = 2 * KEYS * QUERIES * 512
    dma = pltpu.SemaphoreType.DMA
    vmem = pltpu.VMEM
    block = ("P", (32, 16, 128), bf16)
    sent, rows = call(
        pick_body, [("H", batch_rows), ("H", train_embed)],
        [("H", (8, 2, 32, 256), bf16), ("V", (2, 8192), jnp.int32)],
        [vmem((KEYS, 256), bf16), vmem((2, 32, 256), bf16), dma((13,))],
    )
    columns = [[4 * z + chip for z in range(8)] for chip in range(4)]
    column = lax.all_to_all(sent, "train", 0, 0, axis_index_groups=columns, tiled=True)
    flips = []
    for step in range(2):
        own_part = column[:, step].reshape(256, 256)
        flips.append([own_part])
        for flip in range(1, 4):
            flips[step].append(lax.ppermute(own_part, "train", [(t, t ^ flip) for t in range(32)]))
    state = vmem((COLS, KEYS), f32)
    draws = vmem((COLS - 1, KEYS), f32)
    turned_state = ("H", (KEYS, 128), bf16)
    library_total = (QUERIES, 128)
    ahead, base, own, norms, picks, local, library_part = call(
        prep_body,
        [
            ("V", rows), ("H", train_embed), ("H", lib_embed), ("H", labels[None, :]), ("H", prior_draws),
            ("H", noise_draws), ("H", coefficients), ("H", velocity),
        ],
        [
            turned_state, turned_state, ("V", (2, 16, 128), f32), ("V", (1, KEYS), f32), ("V", (512, 256), bf16),
            ("V", (128, 16), jnp.int32), ("H", library_total, f32),
        ],
        [
            vmem((1, KEYS), f32), draws, draws, state, state, vmem((KEYS, 128), bf16), dma((10,)),
            *dense_scratch(QUERIES),
        ],
        flops,
    )
    part_half = call(
        dense_first_body,
        [("H", train_embed), ("A", flips[0][0]), ("A", flips[0][1]), ("H", ahead), ("V", norms)],
        [("V", (16, 16, 128), bf16)], dense_scratch(512), flops // 2,
    )
    part_0 = call(
        dense_rest_body,
        [("H", train_embed), ("A", flips[0][2]), ("A", flips[0][3]), ("H", ahead), ("V", norms), ("V", part_half)],
        [block], dense_scratch(512), flops // 2,
    )
    arrived_0 = exchange(part_0, "train")
    part_1 = call(
        dense_second_body,
        [("H", train_embed), *[("A", part) for part in flips[1]], ("H", base), ("V", norms), ("H", part_0)],
        [("V", (32, 16, 128), bf16)], dense_scratch(QUERIES), flops,
    )
    sent_1 = call(first_body, [("V", arrived_0), ("V", own), ("V", part_1)], [("P", (32, 32, 128), bf16)])
    arrived_1 = exchange(sent_1, "train")
    between, library = call(
        between_body,
        [
            ("V", rows), *[("A", part) for part in flips[0]], ("V", picks), ("V", local), ("H", train_embed),
            ("H", lib_embed), ("H", base), ("V", norms), ("H", library_part), ("H", sent_1),
        ],
        [("V", (256, QUERIES), bf16), ("V", library_total, f32)],
        [vmem((4, 256, 256), bf16), dma((4,)), *dense_scratch(QUERIES)], flops // 2,
    )
    sent_2 = call(
        second_body, [("V", arrived_1), ("V", own), ("V", between)],
        [("P", (8, 144, 128), bf16)], [vmem((QUERIES, HALF), bf16)],
    )
    near = call(
        near_body, [("H", lib_embed), ("V", picks), ("H", sent_2)],
        [("V", (QUERIES, 512), bf16)], [vmem((QUERIES, 256), bf16), dma], flops // 8,
    )
    arrived_2 = exchange(sent_2, "batch")
    sent_3, resid = call(third_body, [("V", arrived_2), ("V", library), ("V", near)], [block, ("V", (512, HALF), f32)])
    arrived_3 = exchange(sent_3, "train")
    new_coef, new_vel = call(
        update_body, [("V", resid), ("V", local), ("V", coefficients), ("V", velocity)],
        [("P", (COLS, KEYS), f32), ("P", (COLS, KEYS), f32)],
    )
    predictions = call(final_body, [("V", arrived_3), ("V", library_prior)], [("P", (32, COLS), f32)])
    return new_coef, new_vel, predictions.T


def solution(mesh):
    return jax.shard_map(
        whole,
        mesh=mesh,
        in_specs=(
            P(),
            P("train", None),
            P("batch", None),
            P("train"),
            P(None, "train"),
            P(None, "train"),
            P(None, "train"),
            P(None, "train"),
            P(None, ("batch", "train")),
        ),
        out_specs=(P(None, "train"), P(None, "train"), P(None, ("batch", "train"))),
        check_vma=False,
    )
```

```python
import jax
import jax.numpy as jnp
from jax import lax
from jax.experimental import pallas as pl
from jax.experimental.pallas import tpu as pltpu
from jax.sharding import PartitionSpec as P


momentum = 0.9
step_rate = 0.1
noise_var = 0.5
noise_scale = 0.7071067811865476
length_sq = 0.088

BETA = (5.0 / (length_sq * 256)) ** 0.5
SCALE = BETA * BETA / 3.0
C1 = 3.0 / BETA
C0 = 3.0 / (BETA * BETA)
RATE = BETA * 1.4426950408889634

CARRY = momentum + momentum * momentum
CUT = step_rate * (1.0 + momentum)

COLS = 33
HALF = 64
KEYS = 4096
QUERIES = 1024
TILE = 512
f32 = jnp.float32
bf16 = jnp.bfloat16

GRANT = 20 << 20


def call(body, ins, outs, scratch=(), flops=0):
    spec = {"H": pl.BlockSpec(memory_space=pltpu.HBM), "V": pl.BlockSpec(memory_space=pltpu.VMEM)}
    spec["P"] = spec["V"]
    spec["A"] = pl.BlockSpec(memory_space=pl.ANY)
    spec["W"] = spec["V"]
    space = {"H": pltpu.HBM, "V": pltpu.VMEM, "P": pltpu.HBM, "A": pl.ANY, "W": pl.ANY}
    kernel = pl.pallas_call(
        body,
        out_shape=[space[kind](shape, dtype) for kind, shape, dtype in outs],
        in_specs=[spec[kind] for kind, _ in ins],
        out_specs=[spec[kind] for kind, _, _ in outs],
        scratch_shapes=list(scratch),
        compiler_params=pltpu.CompilerParams(vmem_limit_bytes=GRANT),
        cost_estimate=pl.CostEstimate(flops=flops, transcendentals=0, bytes_accessed=1 << 20),
    )
    result = kernel(*[pltpu.with_memory_space_constraint(array, space[kind]) for kind, array in ins])
    return result[0] if len(outs) == 1 else result


def places():
    return lax.axis_index("batch"), lax.axis_index("train")


def dot_nt(left, right):
    return lax.dot_general(left, right, (((1,), (1,)), ((), ())), preferred_element_type=f32)


def dot_nn(left, right):
    return jnp.dot(left, right, preferred_element_type=f32)


def two_terms(x):
    high = x.astype(bf16)
    return high, (x - high.astype(f32)).astype(bf16)


def norms_down(x):
    return jnp.sum(jnp.square(x.astype(f32)), axis=1, keepdims=True)


def norms_across(x):
    high, low = two_terms(jnp.square(x.astype(f32)))
    ones = jnp.ones((8, x.shape[1]), bf16)
    return (dot_nt(ones, high) + dot_nt(ones, low))[0:1]


def matern(cross, norms_q, norms_k):
    dist = jnp.maximum((norms_q + norms_k) + cross, 1e-12)
    root = dist * lax.rsqrt(dist)
    return ((root * (root + C1) + C0) * jnp.exp2(root * -RATE)).astype(bf16)


def local_rows(rows_ref, train, groups):
    chunks = []
    for step in range(2):
        for group in groups:
            start = group * QUERIES + (train // 4) * 128
            chunks.append(rows_ref[pl.ds(step, 1), pl.ds(pl.multiple_of(start, 128), 128)])
    while len(chunks) % 8:
        chunks.append(chunks[0])
    stack = jnp.concatenate(chunks, axis=0)
    stack = pltpu.roll(stack, lax.rem(128 - (train % 4) * 32, 128), axis=1)
    return stack - train * KEYS


def one_hot(column, start, width):
    lanes = lax.broadcasted_iota(jnp.int32, (column.shape[0], width), 1)
    return (lanes == column - start).astype(bf16)


def side_by_side(x):
    return jnp.concatenate([x[0:16], x[16:32]], axis=1)


def one_below_other(x):
    return jnp.concatenate([x[:, 0:HALF], x[:, HALF:]], axis=0)


def pack(total, out_ref):
    for place in range(32):
        out_ref[place] = side_by_side(total[32 * place : 32 * place + 32]).astype(bf16)


def pack_flipped(total, train, flips, out_ref):
    own = lax.rem(train, 4)
    for index, flip in enumerate(flips):
        other = lax.bitwise_xor(own, flip)
        for z in range(8):
            start = 256 * index + 32 * z
            out_ref[4 * z + other] = (SCALE * side_by_side(total[start : start + 32, 0:HALF])).astype(bf16)


def pick_body(rows_hbm, embed_hbm, sent_hbm, rows, embed, picked, sems):
    batch, train = places()
    fetch = pltpu.make_async_copy(rows_hbm, rows, sems.at[0])
    fetch.start()
    chunks = []
    for index in range(4):
        part = pl.ds(1024 * index, 1024)
        chunks.append(pltpu.make_async_copy(embed_hbm.at[part], embed.at[part], sems.at[1 + index]))
        chunks[-1].start()
    fetch.wait()
    local = jnp.transpose(local_rows(rows, train, [batch]))
    column = jnp.concatenate([local[0:32, 0:1], local[0:32, 1:2]], axis=0)
    total = jnp.zeros((64, 256), f32)
    for index in range(4):
        chosen = one_hot(column, 1024 * index, 1024)
        chunks[index].wait()
        total = total + dot_nn(chosen, embed[1024 * index : 1024 * index + 1024, :])
    picked[0] = total[0:32].astype(bf16)
    picked[1] = total[32:64].astype(bf16)
    out = [pltpu.make_async_copy(picked, sent_hbm.at[z], sems.at[5 + z]) for z in range(8)]
    for copy in out:
        copy.start()
    for copy in out:
        copy.wait()


def turned(state):
    full = jnp.concatenate([state, jnp.zeros((40 - COLS, KEYS), f32)], axis=0)
    rest = jnp.zeros((128, 128 - 40), f32)
    return [
        jnp.concatenate([jnp.transpose(full[:, 128 * index : 128 * index + 128]), rest], axis=1).astype(bf16)
        for index in range(KEYS // 128)
    ]


def prep_body(
    rows_ref, embed_hbm, library_hbm, labels_hbm, prior_hbm, noise_hbm, coef_hbm, vel_hbm,
    ahead_hbm, base_hbm, own_ref, norms_ref, picks, local_ref, part_hbm,
    labels, prior, noise, coef, vel, ahead_half, sems, *scratch,
):
    embed, query, base_half, query_norms, cross, total, _ = scratch
    batch, train = places()
    copies = [
        pltpu.make_async_copy(source, target, sems.at[index])
        for index, (source, target) in enumerate(
            [
                (coef_hbm, coef), (vel_hbm, vel), (prior_hbm, prior), (noise_hbm, noise), (labels_hbm, labels),
                (embed_hbm, embed), (library_hbm, query),
            ]
        )
    ]
    for copy in copies:
        copy.start()
    mine = jnp.transpose(local_rows(rows_ref, train, [batch]))
    local = jnp.transpose(local_rows(rows_ref, train, range(8)))
    local_ref[...] = local
    for copy in copies[:2]:
        copy.wait()
    ahead = coef[...] + momentum * vel[...]
    base = coef[...] + CARRY * vel[...]
    for index, (one, two) in enumerate(zip(turned(ahead), turned(base))):
        ahead_half[128 * index : 128 * index + 128, :] = one
        base_half[128 * index : 128 * index + 128, :] = two
    out = [
        pltpu.make_async_copy(ahead_half, ahead_hbm, sems.at[7]),
        pltpu.make_async_copy(base_half, base_hbm, sems.at[8]),
    ]
    for copy in out:
        copy.start()
    for copy in copies[2:]:
        copy.wait()
    shift = jnp.concatenate([jnp.zeros((1, KEYS), f32), prior[...] + noise_scale * noise[...]], axis=0)
    targets = labels[...] - shift
    pad = jnp.zeros((HALF - COLS, KEYS), f32)
    for step, state in enumerate((ahead, base)):
        chosen = one_hot(mine[0:32, step : step + 1], 0, KEYS)
        high, low = two_terms(jnp.concatenate([noise_var * state - targets, pad], axis=0))
        own_ref[step] = side_by_side(dot_nt(chosen, high) + dot_nt(chosen, low))
    norms_ref[...] = norms_across(embed[...])
    column = jnp.concatenate([local[0:32, index : index + 1] for index in range(16)], axis=0)
    for index in range(4):
        part = slice(128 * index, 128 * index + 128)
        picks[part, :] = dot_nn(one_hot(column[part], 0, KEYS), embed[...]).astype(bf16)
    total[...] = jnp.zeros_like(total)
    scaled(query, query_norms, slice(0, QUERIES))
    sweep(embed, query, base_half, query_norms, cross, total, norms_ref, (0, LIBRARY_SPLIT), None, True)
    out.append(pltpu.make_async_copy(total, part_hbm, sems.at[9]))
    out[-1].start()
    for copy in out:
        copy.wait()


LIBRARY_SPLIT = 4


def scaled(query, query_norms, part):
    query_norms[part, :] = norms_down(query[part, :])
    query[part, :] = query[part, :] * bf16(-2)


def sweep(embed, query, weight, query_norms, cross, total, norms_ref, tiles, wait, short):
    first, count = tiles

    def keys(index):
        return pl.ds(pl.multiple_of((first + index) * TILE, TILE), TILE)

    def product(index):
        return dot_nt(query[...], embed[keys(index), :])

    def one(index, slot, more):
        if more:
            cross[1 - slot] = product(jnp.minimum(index + 1, count - 1) if short else index + 1)
        value = matern(cross[slot], query_norms[...], norms_ref[:, keys(index)])
        total[...] += dot_nn(value, weight[keys(index), :])

    if wait is not None:
        wait(0)
    cross[0] = product(0)

    def pair(index, carry):
        if wait is not None:
            wait(2 * index + 1)
            if short:
                pl.when(2 * index + 2 < count)(lambda: wait(2 * index + 2))
            else:
                wait(2 * index + 2)
        one(2 * index, 0, True)
        one(2 * index + 1, 1, True)
        return carry

    loops = count // 2 if short else (count - 1) // 2
    lax.fori_loop(0, loops, pair, 0)
    for index in range(2 * loops, count):
        more = index + 1 < count
        if more and wait is not None:
            wait(index + 1)
        one(index, index % 2, more)


def dense_scratch(queries):
    return [
        pltpu.VMEM((KEYS, 256), bf16),
        pltpu.VMEM((queries, 256), bf16),
        pltpu.VMEM((KEYS, 128), bf16),
        pltpu.VMEM((queries, 1), f32),
        pltpu.VMEM((2, queries, TILE), f32),
        pltpu.VMEM((queries, 128), f32),
        pltpu.SemaphoreType.DMA((20,)),
    ]


def dense(embed_hbm, pieces, weight_hbm, norms_ref, scratch, tiles, start_hbm=None, between=None, short=False):
    embed, query, weight, query_norms, cross, total, sems = scratch
    first, count = tiles

    def chunk(index):
        part = pl.ds(pl.multiple_of((first + index) * TILE, TILE), TILE)
        return (
            pltpu.make_async_copy(embed_hbm.at[part], embed.at[part], sems.at[index]),
            pltpu.make_async_copy(weight_hbm.at[part], weight.at[part], sems.at[8 + index]),
        )

    def wait(index):
        for copy in chunk(index):
            copy.wait()

    for index in range(count):
        for copy in chunk(index):
            copy.start()
    rows = query.shape[0] // len(pieces)
    if start_hbm is None:
        total[...] = jnp.zeros_like(total)
        for index, piece in enumerate(pieces):
            part = slice(rows * index, rows * index + rows)
            query_norms[part, :] = norms_down(piece[...])
            query[part, :] = piece[...] * bf16(-2)
    else:
        fetches = [
            pltpu.make_async_copy(pieces[0], query, sems.at[16]), pltpu.make_async_copy(start_hbm, total, sems.at[17])
        ]
        for fetch in fetches:
            fetch.start()
        between()
        for fetch in fetches:
            fetch.wait()
        scaled(query, query_norms, slice(0, rows))
    sweep(embed, query, weight, query_norms, cross, total, norms_ref, tiles, wait, short)
    return total


def dense_first_body(embed, own, flip, weight, norms_ref, out_ref, *scratch):
    total = dense(embed, [own, flip], weight, norms_ref, scratch, (0, 8))
    for index in range(16):
        out_ref[index] = (SCALE * side_by_side(total[32 * index : 32 * index + 32, 0:HALF])).astype(bf16)


def dense_rest_body(embed, flip_2, flip_3, weight, norms_ref, done_ref, out_ref, *scratch):
    train = places()[1]
    own = lax.rem(train, 4)
    for index in range(2):
        other = lax.bitwise_xor(own, index)
        for z in range(8):
            out_ref[4 * z + other] = done_ref[8 * index + z]
    total = dense(embed, [flip_2, flip_3], weight, norms_ref, scratch, (0, 8))
    pack_flipped(total, train, (2, 3), out_ref)


def dense_second_body(embed, flip_0, flip_1, flip_2, flip_3, weight, norms_ref, after, out_ref, *scratch):
    del after
    total = dense(embed, [flip_0, flip_1, flip_2, flip_3], weight, norms_ref, scratch, (0, 8))
    pack_flipped(total, places()[1], range(4), out_ref)


def between_body(
    rows_ref, flip_0, flip_1, flip_2, flip_3, picks, local_ref, embed_hbm, library_hbm, weight_hbm, norms_ref, start_hbm,
    after, between, out_ref, first, sems, *scratch,
):
    del after
    copies = []
    for index, flip in enumerate((flip_0, flip_1, flip_2, flip_3)):
        copies.append(pltpu.make_async_copy(flip, first.at[index], sems.at[index]))
        copies[-1].start()

    def tile():
        batch, train = places()
        column = jnp.concatenate([local_ref[0:32, index : index + 1] for index in range(8, 16)], axis=0)
        mine = local_rows(rows_ref, train, [batch])[0:1, 0:32]
        mine = jnp.concatenate([mine] * 8, axis=1)
        z = lax.broadcasted_iota(jnp.int32, (256, 256), 1) // 32
        same = jnp.where((column == mine) & (z == train // 4), noise_var / SCALE, 0.0)
        second = picks[256:512, :]
        second_norms = norms_down(second)
        second = second * bf16(-2)
        for index, copy in enumerate(copies):
            copy.wait()
            value = matern(dot_nt(second, first[index]), second_norms, norms_across(first[index]))
            if index == 0:
                value = (value.astype(f32) + same).astype(bf16)
            between[:, 256 * index : 256 * index + 256] = value

    tiles = (LIBRARY_SPLIT, 8 - LIBRARY_SPLIT)
    total = dense(embed_hbm, [library_hbm], weight_hbm, norms_ref, scratch, tiles, start_hbm, tile, True)
    out_ref[...] = total[...]


def near_body(library_hbm, picks, after, near, library, sem):
    del after
    copy = pltpu.make_async_copy(library_hbm, library, sem)
    copy.start()
    pick_norms = norms_across(picks[...])
    copy.wait()
    for index in range(2):
        part = slice(512 * index, 512 * index + 512)
        queries = library[part, :]
        near[part, :] = matern(dot_nt(queries * bf16(-2), picks[...]), norms_down(queries), pick_norms)


def first_body(arrived_ref, own_ref, second_ref, out_ref):
    total = own_ref[0]
    for place in range(32):
        total = total + arrived_ref[place].astype(f32)
    total = total.astype(bf16)
    for place in range(32):
        out_ref[place, 0:16, :] = total
        out_ref[place, 16:32, :] = second_ref[place]


def second_body(arrived_ref, own_ref, between, out_ref, resid):
    batch, train = places()
    total = own_ref[1]
    for place in range(32):
        total = total + arrived_ref[place, 16:32, :].astype(f32)
    own = lax.rem(train, 4)
    for flip in range(4):
        other = lax.bitwise_xor(own, flip)
        for z in range(8):
            start = 256 * flip + 32 * z
            resid[start : start + 32, :] = one_below_other(arrived_ref[4 * z + other, 0:16, :])
    mine = one_below_other(total)
    change = dot_nn(between[...], resid[...]) * (-CUT * SCALE)
    group = lax.broadcasted_iota(jnp.int32, (256, HALF), 0) // 32
    change = change + jnp.where(group == batch, jnp.concatenate([mine] * 8, axis=0), 0.0)
    change = jnp.concatenate([change[0:128], change[128:256]], axis=1).astype(bf16)
    kept = arrived_ref[train, 0:16, :]
    for place in range(8):
        out_ref[place, 0:128, :] = change
        out_ref[place, 128:144, :] = kept


def third_body(arrived_ref, library, near, out_ref, resid_ref):
    second = arrived_ref[0, 0:128, :].astype(f32)
    for place in range(1, 8):
        second = second + arrived_ref[place, 0:128, :].astype(f32)
    second = jnp.concatenate([second[:, 0:HALF], second[:, HALF:]], axis=0)
    first = jnp.concatenate([one_below_other(arrived_ref[place, 128:144, :].astype(f32)) for place in range(8)], axis=0)
    resid_ref[...] = jnp.concatenate([first, second], axis=0)
    resid = jnp.concatenate([CUT * first, step_rate * second], axis=0).astype(bf16)
    total = SCALE * (library[:, 0:HALF] - dot_nn(near[...], resid))
    pack(total, out_ref)


def update_body(resid_ref, local_ref, coef_ref, vel_ref, new_coef_ref, new_vel_ref):
    lanes = jnp.concatenate([resid_ref[...], jnp.zeros((512, 128 - HALF), f32)], axis=1)
    across = jnp.transpose(lanes)[0:48]
    grads = []
    for step in range(2):
        column = jnp.concatenate(
            [local_ref[0:32, 8 * step + group : 8 * step + group + 1] for group in range(8)], axis=0
        )
        high, low = two_terms(across[:, 256 * step : 256 * step + 256])
        chosen = one_hot(column, 0, KEYS)
        grads.append((dot_nn(high, chosen) + dot_nn(low, chosen))[0:COLS])
    vel = momentum * vel_ref[...] - step_rate * grads[0]
    coef = coef_ref[...] + vel
    vel = momentum * vel - step_rate * grads[1]
    new_vel_ref[...] = vel
    new_coef_ref[...] = coef + vel


def final_body(arrived_ref, prior_ref, out_ref):
    total = arrived_ref[0].astype(f32)
    for place in range(1, 32):
        total = total + arrived_ref[place].astype(f32)
    total = one_below_other(total)[:, 0:COLS]
    out_ref[...] = total + jnp.concatenate([jnp.zeros((32, 1), f32), jnp.transpose(prior_ref[...])], axis=1)


def exchange(x, axis):
    return lax.all_to_all(x, axis, split_axis=0, concat_axis=0, tiled=True)


def whole(
    batch_rows, train_embed, lib_embed, labels, prior_draws, noise_draws, coefficients, velocity, library_prior
):
    flops = 2 * KEYS * QUERIES * 512
    dma = pltpu.SemaphoreType.DMA
    vmem = pltpu.VMEM
    block = ("P", (32, 16, 128), bf16)
    sent, rows = call(
        pick_body, [("H", batch_rows), ("H", train_embed)],
        [("H", (8, 2, 32, 256), bf16), ("V", (2, 8192), jnp.int32)],
        [vmem((KEYS, 256), bf16), vmem((2, 32, 256), bf16), dma((13,))],
    )
    columns = [[4 * z + chip for z in range(8)] for chip in range(4)]
    column = lax.all_to_all(sent, "train", 0, 0, axis_index_groups=columns, tiled=True)
    flips = []
    for step in range(2):
        own_part = column[:, step].reshape(256, 256)
        flips.append([own_part])
        for flip in range(1, 4):
            flips[step].append(lax.ppermute(own_part, "train", [(t, t ^ flip) for t in range(32)]))
    state = vmem((COLS, KEYS), f32)
    draws = vmem((COLS - 1, KEYS), f32)
    turned_state = ("H", (KEYS, 128), bf16)
    library_total = (QUERIES, 128)
    ahead, base, own, norms, picks, local, library_part = call(
        prep_body,
        [
            ("V", rows), ("H", train_embed), ("H", lib_embed), ("H", labels[None, :]), ("H", prior_draws),
            ("H", noise_draws), ("H", coefficients), ("H", velocity),
        ],
        [
            turned_state, turned_state, ("V", (2, 16, 128), f32), ("V", (1, KEYS), f32), ("V", (512, 256), bf16),
            ("V", (128, 16), jnp.int32), ("H", library_total, f32),
        ],
        [
            vmem((1, KEYS), f32), draws, draws, state, state, vmem((KEYS, 128), bf16), dma((10,)),
            *dense_scratch(QUERIES),
        ],
        flops,
    )
    part_half = call(
        dense_first_body,
        [("H", train_embed), ("W", flips[0][0]), ("W", flips[0][1]), ("H", ahead), ("V", norms)],
        [("V", (16, 16, 128), bf16)], dense_scratch(512), flops // 2,
    )
    part_0 = call(
        dense_rest_body,
        [("H", train_embed), ("W", flips[0][2]), ("W", flips[0][3]), ("H", ahead), ("V", norms), ("V", part_half)],
        [block], dense_scratch(512), flops // 2,
    )
    arrived_0 = exchange(part_0, "train")
    part_1 = call(
        dense_second_body,
        [("H", train_embed), *[("W", part) for part in flips[1]], ("H", base), ("V", norms), ("H", part_0)],
        [("V", (32, 16, 128), bf16)], dense_scratch(QUERIES), flops,
    )
    sent_1 = call(first_body, [("V", arrived_0), ("V", own), ("V", part_1)], [("P", (32, 32, 128), bf16)])
    arrived_1 = exchange(sent_1, "train")
    between, library = call(
        between_body,
        [
            ("V", rows), *[("A", part) for part in flips[0]], ("V", picks), ("V", local), ("H", train_embed),
            ("H", lib_embed), ("H", base), ("V", norms), ("H", library_part), ("H", sent_1),
        ],
        [("V", (256, QUERIES), bf16), ("V", library_total, f32)],
        [vmem((4, 256, 256), bf16), dma((4,)), *dense_scratch(QUERIES)], flops // 2,
    )
    sent_2 = call(
        second_body, [("V", arrived_1), ("V", own), ("V", between)],
        [("P", (8, 144, 128), bf16)], [vmem((QUERIES, HALF), bf16)],
    )
    near = call(
        near_body, [("H", lib_embed), ("V", picks), ("H", sent_2)],
        [("V", (QUERIES, 512), bf16)], [vmem((QUERIES, 256), bf16), dma], flops // 8,
    )
    arrived_2 = exchange(sent_2, "batch")
    sent_3, resid = call(third_body, [("V", arrived_2), ("V", library), ("V", near)], [block, ("V", (512, HALF), f32)])
    arrived_3 = exchange(sent_3, "train")
    new_coef, new_vel = call(
        update_body, [("V", resid), ("V", local), ("V", coefficients), ("V", velocity)],
        [("P", (COLS, KEYS), f32), ("P", (COLS, KEYS), f32)],
    )
    predictions = call(final_body, [("V", arrived_3), ("V", library_prior)], [("P", (32, COLS), f32)])
    return new_coef, new_vel, predictions.T


def solution(mesh):
    return jax.shard_map(
        whole,
        mesh=mesh,
        in_specs=(
            P(),
            P("train", None),
            P("batch", None),
            P("train"),
            P(None, "train"),
            P(None, "train"),
            P(None, "train"),
            P(None, "train"),
            P(None, ("batch", "train")),
        ),
        out_specs=(P(None, "train"), P(None, "train"), P(None, ("batch", "train"))),
        check_vma=False,
    )
```

```python
import jax
import jax.numpy as jnp
from jax import lax
from jax.experimental import pallas as pl
from jax.experimental.pallas import tpu as pltpu
from jax.sharding import PartitionSpec as P


momentum = 0.9
step_rate = 0.1
noise_var = 0.5
noise_scale = 0.7071067811865476
length_sq = 0.088

BETA = (5.0 / (length_sq * 256)) ** 0.5
SCALE = BETA * BETA / 3.0
C1 = 3.0 / BETA
C0 = 3.0 / (BETA * BETA)
RATE = BETA * 1.4426950408889634

CARRY = momentum + momentum * momentum
CUT = step_rate * (1.0 + momentum)

COLS = 33
HALF = 64
KEYS = 4096
QUERIES = 1024
TILE = 512
f32 = jnp.float32
bf16 = jnp.bfloat16

GRANT = 20 << 20


def call(body, ins, outs, scratch=(), flops=0):
    spec = {"H": pl.BlockSpec(memory_space=pltpu.HBM), "V": pl.BlockSpec(memory_space=pltpu.VMEM)}
    spec["P"] = spec["V"]
    spec["A"] = pl.BlockSpec(memory_space=pl.ANY)
    spec["W"] = spec["V"]
    space = {"H": pltpu.HBM, "V": pltpu.VMEM, "P": pltpu.HBM, "A": pl.ANY, "W": pl.ANY}
    kernel = pl.pallas_call(
        body,
        out_shape=[space[kind](shape, dtype) for kind, shape, dtype in outs],
        in_specs=[spec[kind] for kind, _ in ins],
        out_specs=[spec[kind] for kind, _, _ in outs],
        scratch_shapes=list(scratch),
        compiler_params=pltpu.CompilerParams(vmem_limit_bytes=GRANT),
        cost_estimate=pl.CostEstimate(flops=flops, transcendentals=0, bytes_accessed=1 << 20),
    )
    result = kernel(*[pltpu.with_memory_space_constraint(array, space[kind]) for kind, array in ins])
    return result[0] if len(outs) == 1 else result


def places():
    return lax.axis_index("batch"), lax.axis_index("train")


def dot_nt(left, right):
    return lax.dot_general(left, right, (((1,), (1,)), ((), ())), preferred_element_type=f32)


def dot_nn(left, right):
    return jnp.dot(left, right, preferred_element_type=f32)


def two_terms(x):
    high = x.astype(bf16)
    return high, (x - high.astype(f32)).astype(bf16)


def norms_down(x):
    return jnp.sum(jnp.square(x.astype(f32)), axis=1, keepdims=True)


def norms_across(x):
    high, low = two_terms(jnp.square(x.astype(f32)))
    ones = jnp.ones((8, x.shape[1]), bf16)
    return (dot_nt(ones, high) + dot_nt(ones, low))[0:1]


def matern(cross, norms_q, norms_k):
    dist = jnp.maximum((norms_q + norms_k) + cross, 1e-12)
    root = dist * lax.rsqrt(dist)
    return ((root * (root + C1) + C0) * jnp.exp2(root * -RATE)).astype(bf16)


def local_rows(rows_ref, train, groups):
    chunks = []
    for step in range(2):
        for group in groups:
            start = group * QUERIES + (train // 4) * 128
            chunks.append(rows_ref[pl.ds(step, 1), pl.ds(pl.multiple_of(start, 128), 128)])
    while len(chunks) % 8:
        chunks.append(chunks[0])
    stack = jnp.concatenate(chunks, axis=0)
    stack = pltpu.roll(stack, lax.rem(128 - (train % 4) * 32, 128), axis=1)
    return stack - train * KEYS


def one_hot(column, start, width):
    lanes = lax.broadcasted_iota(jnp.int32, (column.shape[0], width), 1)
    return (lanes == column - start).astype(bf16)


def side_by_side(x):
    return jnp.concatenate([x[0:16], x[16:32]], axis=1)


def one_below_other(x):
    return jnp.concatenate([x[:, 0:HALF], x[:, HALF:]], axis=0)


def tight(x):
    bands = [x[8 * band : 8 * band + 8] for band in range(4)]
    main = jnp.concatenate([band[:, 0:32] for band in bands], axis=1)
    last = jnp.concatenate([*[band[:, 32:33] for band in bands], jnp.zeros((8, 124), f32)], axis=1)
    return main, last


def loose(main, last):
    rest = jnp.zeros((8, 31), f32)
    return jnp.concatenate(
        [
            jnp.concatenate([main[:, 32 * band : 32 * band + 32], last[:, band : band + 1], rest], axis=1)
            for band in range(4)
        ],
        axis=0,
    )


def pack(total, out_ref):
    for place in range(32):
        out_ref[place] = side_by_side(total[32 * place : 32 * place + 32]).astype(bf16)


def pack_flipped(total, train, flips, out_ref):
    own = lax.rem(train, 4)
    for index, flip in enumerate(flips):
        other = lax.bitwise_xor(own, flip)
        for z in range(8):
            start = 256 * index + 32 * z
            out_ref[4 * z + other] = (SCALE * side_by_side(total[start : start + 32, 0:HALF])).astype(bf16)


def pick_body(rows_hbm, embed_hbm, sent_hbm, rows, embed, picked, sems):
    batch, train = places()
    fetch = pltpu.make_async_copy(rows_hbm, rows, sems.at[0])
    fetch.start()
    chunks = []
    for index in range(4):
        part = pl.ds(1024 * index, 1024)
        chunks.append(pltpu.make_async_copy(embed_hbm.at[part], embed.at[part], sems.at[1 + index]))
        chunks[-1].start()
    fetch.wait()
    local = jnp.transpose(local_rows(rows, train, [batch]))
    column = jnp.concatenate([local[0:32, 0:1], local[0:32, 1:2]], axis=0)
    total = jnp.zeros((64, 256), f32)
    for index in range(4):
        chosen = one_hot(column, 1024 * index, 1024)
        chunks[index].wait()
        total = total + dot_nn(chosen, embed[1024 * index : 1024 * index + 1024, :])
    picked[0] = total[0:32].astype(bf16)
    picked[1] = total[32:64].astype(bf16)
    out = [pltpu.make_async_copy(picked, sent_hbm.at[z], sems.at[5 + z]) for z in range(8)]
    for copy in out:
        copy.start()
    for copy in out:
        copy.wait()


def turned(state):
    full = jnp.concatenate([state, jnp.zeros((40 - COLS, KEYS), f32)], axis=0)
    rest = jnp.zeros((128, 128 - 40), f32)
    return [
        jnp.concatenate([jnp.transpose(full[:, 128 * index : 128 * index + 128]), rest], axis=1).astype(bf16)
        for index in range(KEYS // 128)
    ]


def prep_body(
    rows_ref, embed_hbm, library_hbm, labels_hbm, prior_hbm, noise_hbm, coef_hbm, vel_hbm,
    ahead_hbm, base_hbm, own_ref, norms_ref, picks, local_ref, part_hbm,
    labels, prior, noise, coef, vel, ahead_half, sems, *scratch,
):
    embed, query, base_half, query_norms, cross, total, _ = scratch
    batch, train = places()
    copies = [
        pltpu.make_async_copy(source, target, sems.at[index])
        for index, (source, target) in enumerate(
            [
                (coef_hbm, coef), (vel_hbm, vel), (prior_hbm, prior), (noise_hbm, noise), (labels_hbm, labels),
                (embed_hbm, embed), (library_hbm, query),
            ]
        )
    ]
    for copy in copies:
        copy.start()
    mine = jnp.transpose(local_rows(rows_ref, train, [batch]))
    local = jnp.transpose(local_rows(rows_ref, train, range(8)))
    local_ref[...] = local
    for copy in copies[:2]:
        copy.wait()
    ahead = coef[...] + momentum * vel[...]
    base = coef[...] + CARRY * vel[...]
    for index, (one, two) in enumerate(zip(turned(ahead), turned(base))):
        ahead_half[128 * index : 128 * index + 128, :] = one
        base_half[128 * index : 128 * index + 128, :] = two
    out = [
        pltpu.make_async_copy(ahead_half, ahead_hbm, sems.at[7]),
        pltpu.make_async_copy(base_half, base_hbm, sems.at[8]),
    ]
    for copy in out:
        copy.start()
    for copy in copies[2:]:
        copy.wait()
    shift = jnp.concatenate([jnp.zeros((1, KEYS), f32), prior[...] + noise_scale * noise[...]], axis=0)
    targets = labels[...] - shift
    pad = jnp.zeros((HALF - COLS, KEYS), f32)
    for step, state in enumerate((ahead, base)):
        chosen = one_hot(mine[0:32, step : step + 1], 0, KEYS)
        high, low = two_terms(jnp.concatenate([noise_var * state - targets, pad], axis=0))
        own_ref[step] = side_by_side(dot_nt(chosen, high) + dot_nt(chosen, low))
    norms_ref[...] = norms_across(embed[...])
    column = jnp.concatenate([local[0:32, index : index + 1] for index in range(16)], axis=0)
    for index in range(4):
        part = slice(128 * index, 128 * index + 128)
        picks[part, :] = dot_nn(one_hot(column[part], 0, KEYS), embed[...]).astype(bf16)
    total[...] = jnp.zeros_like(total)
    scaled(query, query_norms, slice(0, QUERIES))
    sweep(embed, query, base_half, query_norms, cross, total, norms_ref, (0, LIBRARY_SPLIT), None, True)
    out.append(pltpu.make_async_copy(total, part_hbm, sems.at[9]))
    out[-1].start()
    for copy in out:
        copy.wait()


LIBRARY_SPLIT = 4


def scaled(query, query_norms, part):
    query_norms[part, :] = norms_down(query[part, :])
    query[part, :] = query[part, :] * bf16(-2)


def sweep(embed, query, weight, query_norms, cross, total, norms_ref, tiles, wait, short):
    first, count = tiles

    def keys(index):
        return pl.ds(pl.multiple_of((first + index) * TILE, TILE), TILE)

    def product(index):
        return dot_nt(query[...], embed[keys(index), :])

    def one(index, slot, more):
        if more:
            cross[1 - slot] = product(jnp.minimum(index + 1, count - 1) if short else index + 1)
        value = matern(cross[slot], query_norms[...], norms_ref[:, keys(index)])
        total[...] += dot_nn(value, weight[keys(index), :])

    if wait is not None:
        wait(0)
    cross[0] = product(0)

    def pair(index, carry):
        if wait is not None:
            wait(2 * index + 1)
            if short:
                pl.when(2 * index + 2 < count)(lambda: wait(2 * index + 2))
            else:
                wait(2 * index + 2)
        one(2 * index, 0, True)
        one(2 * index + 1, 1, True)
        return carry

    loops = count // 2 if short else (count - 1) // 2
    lax.fori_loop(0, loops, pair, 0)
    for index in range(2 * loops, count):
        more = index + 1 < count
        if more and wait is not None:
            wait(index + 1)
        one(index, index % 2, more)


def dense_scratch(queries):
    return [
        pltpu.VMEM((KEYS, 256), bf16),
        pltpu.VMEM((queries, 256), bf16),
        pltpu.VMEM((KEYS, 128), bf16),
        pltpu.VMEM((queries, 1), f32),
        pltpu.VMEM((2, queries, TILE), f32),
        pltpu.VMEM((queries, 128), f32),
        pltpu.SemaphoreType.DMA((20,)),
    ]


def dense(embed_hbm, pieces, weight_hbm, norms_ref, scratch, tiles, start_hbm=None, between=None, short=False):
    embed, query, weight, query_norms, cross, total, sems = scratch
    first, count = tiles

    def chunk(index):
        part = pl.ds(pl.multiple_of((first + index) * TILE, TILE), TILE)
        return (
            pltpu.make_async_copy(embed_hbm.at[part], embed.at[part], sems.at[index]),
            pltpu.make_async_copy(weight_hbm.at[part], weight.at[part], sems.at[8 + index]),
        )

    def wait(index):
        for copy in chunk(index):
            copy.wait()

    for index in range(count):
        for copy in chunk(index):
            copy.start()
    rows = query.shape[0] // len(pieces)
    if start_hbm is None:
        total[...] = jnp.zeros_like(total)
        for index, piece in enumerate(pieces):
            part = slice(rows * index, rows * index + rows)
            query_norms[part, :] = norms_down(piece[...])
            query[part, :] = piece[...] * bf16(-2)
    else:
        fetches = [
            pltpu.make_async_copy(pieces[0], query, sems.at[16]), pltpu.make_async_copy(start_hbm, total, sems.at[17])
        ]
        for fetch in fetches:
            fetch.start()
        between()
        for fetch in fetches:
            fetch.wait()
        scaled(query, query_norms, slice(0, rows))
    sweep(embed, query, weight, query_norms, cross, total, norms_ref, tiles, wait, short)
    return total


def dense_first_body(embed, own, flip, weight, norms_ref, out_ref, *scratch):
    total = dense(embed, [own, flip], weight, norms_ref, scratch, (0, 8))
    for index in range(16):
        out_ref[index] = (SCALE * side_by_side(total[32 * index : 32 * index + 32, 0:HALF])).astype(bf16)


def dense_rest_body(embed, flip_2, flip_3, weight, norms_ref, done_ref, out_ref, *scratch):
    train = places()[1]
    own = lax.rem(train, 4)
    for index in range(2):
        other = lax.bitwise_xor(own, index)
        for z in range(8):
            out_ref[4 * z + other] = done_ref[8 * index + z]
    total = dense(embed, [flip_2, flip_3], weight, norms_ref, scratch, (0, 8))
    pack_flipped(total, train, (2, 3), out_ref)


def dense_second_body(embed, flip_0, flip_1, flip_2, flip_3, weight, norms_ref, after, out_ref, *scratch):
    del after
    total = dense(embed, [flip_0, flip_1, flip_2, flip_3], weight, norms_ref, scratch, (0, 8))
    own = lax.rem(places()[1], 4)
    for flip in range(4):
        other = lax.bitwise_xor(own, flip)
        for z in range(8):
            start = 256 * flip + 32 * z
            main, last = tight(SCALE * total[start : start + 32, 0:HALF])
            out_ref[4 * z + other] = jnp.concatenate([main, last], axis=0)


def between_body(
    rows_ref, flip_0, flip_1, flip_2, flip_3, picks, local_ref, embed_hbm, library_hbm, weight_hbm, norms_ref, start_hbm,
    after, between, out_ref, first, sems, *scratch,
):
    del after
    copies = []
    for index, flip in enumerate((flip_0, flip_1, flip_2, flip_3)):
        copies.append(pltpu.make_async_copy(flip, first.at[index], sems.at[index]))
        copies[-1].start()

    def tile():
        batch, train = places()
        column = jnp.concatenate([local_ref[0:32, index : index + 1] for index in range(8, 16)], axis=0)
        mine = local_rows(rows_ref, train, [batch])[0:1, 0:32]
        mine = jnp.concatenate([mine] * 8, axis=1)
        z = lax.broadcasted_iota(jnp.int32, (256, 256), 1) // 32
        same = jnp.where((column == mine) & (z == train // 4), noise_var / SCALE, 0.0)
        second = picks[256:512, :]
        second_norms = norms_down(second)
        second = second * bf16(-2)
        for index, copy in enumerate(copies):
            copy.wait()
            value = matern(dot_nt(second, first[index]), second_norms, norms_across(first[index]))
            if index == 0:
                value = (value.astype(f32) + same).astype(bf16)
            between[:, 256 * index : 256 * index + 256] = value

    tiles = (LIBRARY_SPLIT, 8 - LIBRARY_SPLIT)
    total = dense(embed_hbm, [library_hbm], weight_hbm, norms_ref, scratch, tiles, start_hbm, tile, True)
    out_ref[...] = total[...]


def near_body(library_hbm, picks, after, near, library, sem):
    del after
    copy = pltpu.make_async_copy(library_hbm, library, sem)
    copy.start()
    pick_norms = norms_across(picks[...])
    copy.wait()
    for index in range(2):
        part = slice(512 * index, 512 * index + 512)
        queries = library[part, :]
        near[part, :] = matern(dot_nt(queries * bf16(-2), picks[...]), norms_down(queries), pick_norms)


def first_body(arrived_ref, own_ref, second_ref, out_ref):
    total = own_ref[0]
    for place in range(32):
        total = total + arrived_ref[place].astype(f32)
    main, last = tight(one_below_other(total))
    lane = lax.broadcasted_iota(jnp.int32, (8, 128), 1)
    for place in range(32):
        other = pltpu.roll(second_ref[place, 8:16, :], 4, axis=1)
        out_ref[place] = jnp.concatenate(
            [main, second_ref[place, 0:8, :], jnp.where(lane < 4, last, other)], axis=0
        ).astype(bf16)


def second_body(arrived_ref, own_ref, between, out_ref, resid):
    batch, train = places()
    mains = jnp.zeros((8, 128), f32)
    lasts = jnp.zeros((8, 128), f32)
    for place in range(32):
        mains = mains + arrived_ref[place, 8:16, :].astype(f32)
        lasts = lasts + arrived_ref[place, 16:24, :].astype(f32)
    mine = one_below_other(own_ref[1]) + loose(mains, pltpu.roll(lasts, 124, axis=1))
    own = lax.rem(train, 4)
    for flip in range(4):
        other = lax.bitwise_xor(own, flip)
        for z in range(8):
            start = 256 * flip + 32 * z
            block = arrived_ref[4 * z + other].astype(f32)
            resid[start : start + 32, :] = loose(block[0:8], block[16:24]).astype(bf16)
    change = dot_nn(between[...], resid[...]) * (-CUT * SCALE)
    group = lax.broadcasted_iota(jnp.int32, (256, HALF), 0) // 32
    change = change + jnp.where(group == batch, jnp.concatenate([mine] * 8, axis=0), 0.0)
    change = jnp.concatenate([change[0:128], change[128:256]], axis=1).astype(bf16)
    kept = resid[pl.ds(pl.multiple_of((train // 4) * 32, 32), 32), :].astype(f32)
    kept = side_by_side(kept).astype(bf16)
    for place in range(8):
        out_ref[place, 0:128, :] = change
        out_ref[place, 128:144, :] = kept


def third_body(arrived_ref, library, near, out_ref, resid_ref):
    second = arrived_ref[0, 0:128, :].astype(f32)
    for place in range(1, 8):
        second = second + arrived_ref[place, 0:128, :].astype(f32)
    second = jnp.concatenate([second[:, 0:HALF], second[:, HALF:]], axis=0)
    first = jnp.concatenate([one_below_other(arrived_ref[place, 128:144, :].astype(f32)) for place in range(8)], axis=0)
    resid_ref[...] = jnp.concatenate([first, second], axis=0)
    resid = jnp.concatenate([CUT * first, step_rate * second], axis=0).astype(bf16)
    total = SCALE * (library[:, 0:HALF] - dot_nn(near[...], resid))
    pack(total, out_ref)


def update_body(resid_ref, local_ref, coef_ref, vel_ref, new_coef_ref, new_vel_ref):
    lanes = jnp.concatenate([resid_ref[...], jnp.zeros((512, 128 - HALF), f32)], axis=1)
    across = jnp.transpose(lanes)[0:48]
    grads = []
    for step in range(2):
        column = jnp.concatenate(
            [local_ref[0:32, 8 * step + group : 8 * step + group + 1] for group in range(8)], axis=0
        )
        high, low = two_terms(across[:, 256 * step : 256 * step + 256])
        chosen = one_hot(column, 0, KEYS)
        grads.append((dot_nn(high, chosen) + dot_nn(low, chosen))[0:COLS])
    vel = momentum * vel_ref[...] - step_rate * grads[0]
    coef = coef_ref[...] + vel
    vel = momentum * vel - step_rate * grads[1]
    new_vel_ref[...] = vel
    new_coef_ref[...] = coef + vel


def final_body(arrived_ref, prior_ref, out_ref):
    total = arrived_ref[0].astype(f32)
    for place in range(1, 32):
        total = total + arrived_ref[place].astype(f32)
    total = one_below_other(total)[:, 0:COLS]
    out_ref[...] = total + jnp.concatenate([jnp.zeros((32, 1), f32), jnp.transpose(prior_ref[...])], axis=1)


def exchange(x, axis):
    return lax.all_to_all(x, axis, split_axis=0, concat_axis=0, tiled=True)


def whole(
    batch_rows, train_embed, lib_embed, labels, prior_draws, noise_draws, coefficients, velocity, library_prior
):
    flops = 2 * KEYS * QUERIES * 512
    dma = pltpu.SemaphoreType.DMA
    vmem = pltpu.VMEM
    block = ("P", (32, 16, 128), bf16)
    sent, rows = call(
        pick_body, [("H", batch_rows), ("H", train_embed)],
        [("H", (8, 2, 32, 256), bf16), ("V", (2, 8192), jnp.int32)],
        [vmem((KEYS, 256), bf16), vmem((2, 32, 256), bf16), dma((13,))],
    )
    columns = [[4 * z + chip for z in range(8)] for chip in range(4)]
    column = lax.all_to_all(sent, "train", 0, 0, axis_index_groups=columns, tiled=True)
    flips = []
    for step in range(2):
        own_part = column[:, step].reshape(256, 256)
        flips.append([own_part])
        for flip in range(1, 4):
            flips[step].append(lax.ppermute(own_part, "train", [(t, t ^ flip) for t in range(32)]))
    state = vmem((COLS, KEYS), f32)
    draws = vmem((COLS - 1, KEYS), f32)
    turned_state = ("H", (KEYS, 128), bf16)
    library_total = (QUERIES, 128)
    ahead, base, own, norms, picks, local, library_part = call(
        prep_body,
        [
            ("V", rows), ("H", train_embed), ("H", lib_embed), ("H", labels[None, :]), ("H", prior_draws),
            ("H", noise_draws), ("H", coefficients), ("H", velocity),
        ],
        [
            turned_state, turned_state, ("V", (2, 16, 128), f32), ("V", (1, KEYS), f32), ("V", (512, 256), bf16),
            ("V", (128, 16), jnp.int32), ("H", library_total, f32),
        ],
        [
            vmem((1, KEYS), f32), draws, draws, state, state, vmem((KEYS, 128), bf16), dma((10,)),
            *dense_scratch(QUERIES),
        ],
        flops,
    )
    part_half = call(
        dense_first_body,
        [("H", train_embed), ("W", flips[0][0]), ("W", flips[0][1]), ("H", ahead), ("V", norms)],
        [("V", (16, 16, 128), bf16)], dense_scratch(512), flops // 2,
    )
    part_0 = call(
        dense_rest_body,
        [("H", train_embed), ("W", flips[0][2]), ("W", flips[0][3]), ("H", ahead), ("V", norms), ("V", part_half)],
        [block], dense_scratch(512), flops // 2,
    )
    arrived_0 = exchange(part_0, "train")
    part_1 = call(
        dense_second_body,
        [("H", train_embed), *[("W", part) for part in flips[1]], ("H", base), ("V", norms), ("H", part_0)],
        [("V", (32, 16, 128), f32)], dense_scratch(QUERIES), flops,
    )
    sent_1 = call(first_body, [("V", arrived_0), ("V", own), ("V", part_1)], [("P", (32, 24, 128), bf16)])
    arrived_1 = exchange(sent_1, "train")
    between, library = call(
        between_body,
        [
            ("V", rows), *[("A", part) for part in flips[0]], ("V", picks), ("V", local), ("H", train_embed),
            ("H", lib_embed), ("H", base), ("V", norms), ("H", library_part), ("H", sent_1),
        ],
        [("V", (256, QUERIES), bf16), ("V", library_total, f32)],
        [vmem((4, 256, 256), bf16), dma((4,)), *dense_scratch(QUERIES)], flops // 2,
    )
    sent_2 = call(
        second_body, [("V", arrived_1), ("V", own), ("V", between)],
        [("P", (8, 144, 128), bf16)], [vmem((QUERIES, HALF), bf16)],
    )
    near = call(
        near_body, [("H", lib_embed), ("V", picks), ("H", sent_2)],
        [("V", (QUERIES, 512), bf16)], [vmem((QUERIES, 256), bf16), dma], flops // 8,
    )
    arrived_2 = exchange(sent_2, "batch")
    sent_3, resid = call(third_body, [("V", arrived_2), ("V", library), ("V", near)], [block, ("V", (512, HALF), f32)])
    arrived_3 = exchange(sent_3, "train")
    new_coef, new_vel = call(
        update_body, [("V", resid), ("V", local), ("V", coefficients), ("V", velocity)],
        [("P", (COLS, KEYS), f32), ("P", (COLS, KEYS), f32)],
    )
    predictions = call(final_body, [("V", arrived_3), ("V", library_prior)], [("P", (32, COLS), f32)])
    return new_coef, new_vel, predictions.T


def solution(mesh):
    return jax.shard_map(
        whole,
        mesh=mesh,
        in_specs=(
            P(),
            P("train", None),
            P("batch", None),
            P("train"),
            P(None, "train"),
            P(None, "train"),
            P(None, "train"),
            P(None, "train"),
            P(None, ("batch", "train")),
        ),
        out_specs=(P(None, "train"), P(None, "train"), P(None, ("batch", "train"))),
        check_vma=False,
    )
```
